32 devices in a mesh: seq: 8 (over y, x, core), head: 4 (over z).
Axes of the slice: x: 2, y: 2, z: 4, core: 2. Of those that a mesh axis runs over, the one named last changes fastest.
Arguments:
- hidden_in: bfloat16 [4096, 1024], P('seq', 'head'), may hold values from -6 to 6
- out_grad: bfloat16 [4096, 1024], P('seq', 'head'), may hold values from -6 to 6
- norm_gain: float32 [1024], replicated, may hold values from 0.1 to 1.9
- gate_weight: bfloat16 [1024, 2048], P(None, 'head'), may hold values from -0.1875 to 0.1875
- value_weight: bfloat16 [1024, 2048], P(None, 'head'), may hold values from -0.1875 to 0.1875
- step_weight: bfloat16 [1024, 32], P(None, 'head'), may hold values from -0.375 to 0.375
- state_weight: bfloat16 [1024, 256], replicated, may hold values from -0.1875 to 0.1875
- value_taps: float32 [4, 2048], P(None, 'head'), may hold values from -3 to 3
- value_bias: float32 [2048], P('head'), may hold values from -0.5 to 0.5
- state_taps: float32 [4, 256], replicated, may hold values from -3 to 3
- state_bias: float32 [256], replicated, may hold values from -0.5 to 0.5
- step_bias: float32 [32], P('head'), may hold values from -14 to 1, as said below
- decay_log: float32 [32], P('head'), may hold values from -4 to -1, as said below
- skip_gain: float32 [32], P('head'), may hold values from 0.5 to 2
- gate_gain: float32 [2048], P('head'), may hold values from 0.1 to 1.9
- out_weight: bfloat16 [2048, 1024], P('head'), may hold values from -0.125 to 0.125
Outputs:
- block_out: bfloat16 [4096, 1024], P('seq', 'head')
- grad_in: bfloat16 [4096, 1024], P('seq', 'head')
- grad_norm_gain: float32 [1024], replicated
- grad_gate_weight: float32 [1024, 2048], P('seq', 'head')
- grad_value_weight: float32 [1024, 2048], P('seq', 'head')
- grad_step_weight: float32 [1024, 32], P('seq', 'head')
- grad_state_weight: float32 [1024, 256], P(('seq', 'head'))
- grad_value_taps: float32 [4, 2048], P(None, 'head')
- grad_value_bias: float32 [2048], P('head')
- grad_state_taps: float32 [4, 256], replicated
- grad_state_bias: float32 [256], replicated
- grad_step_bias: float32 [32], P('head')
- grad_decay_log: float32 [32], P('head')
- grad_skip_gain: float32 [32], P('head')
- grad_gate_gain: float32 [2048], P('head')
- grad_out_weight: float32 [2048, 1024], P('head', 'seq')
The draws below stay inside these ranges and needn't reach their ends.
Inputs may be any that keep to these rules, and one draw needn't show every extreme that they name: `step_bias`: one bias per head. `decay_log`: one value per head.
All inputs are finite; a program needn't handle non-finite values.
Results may differ from the reference program's by a relative error of at most 0.012.
The reference program's roundings to bfloat16 on the way count: a program that leaves them out, or rounds other values in their place, can miss the bound.
Values may be sent and summed in bfloat16 or wider, within the bound.
No kernel may reach another device: no remote copies, remote signals or barrier semaphores. Data moves between devices by JAX's collectives and lax.ppermute only.
A program may use at most 128 MiB of HBM per device.

```python
import math
import jax
import jax.numpy as jnp
from jax import lax

D = 1024
HEADS = 32
HEAD_DIM = 64
STATE = 128
CONV = 4
SPAN = 256
TOK_DEV = 512
D_INNER = 2048
TOKENS = 4096


def head_rates(key):
    base = jax.random.fold_in(key, 11)
    first, second, third, fourth, fifth = jax.random.split(base, 5)
    classes = jax.random.randint(first, (HEADS,), 0, 3)
    fast_heads = (classes == 0).astype(jnp.float32)
    middle_heads = (classes == 1).astype(jnp.float32)
    slow_heads = 1.0 - fast_heads - middle_heads
    slow_rate = math.log(10.0) / TOKENS * jax.random.uniform(second, (HEADS,), jnp.float32, 0.2, 0.8)
    fast_rate = jax.random.uniform(third, (HEADS,), jnp.float32, 1.0 / 50.0, 1.0 / 30.0)
    middle_rate = jax.random.uniform(fifth, (HEADS,), jnp.float32, 0.7, 2.0) / TOK_DEV
    decay_rate = slow_heads * slow_rate + middle_heads * middle_rate + fast_heads * fast_rate
    strength = jnp.exp(jax.random.uniform(fourth, (HEADS,), jnp.float32, math.log(0.03), math.log(0.3)))
    step_size = decay_rate / strength
    return (step_size, strength)


def draw_step_bias(key, part):
    step_size, strength = head_rates(key)
    return jnp.log(jnp.expm1(step_size * math.exp(-2.0)))


def draw_decay_log(key, part):
    step_size, strength = head_rates(key)
    return jnp.log(strength)


def spiked(entries, key, source, target, blocks, factor):
    def block_of(position):
        return (jnp.arange(entries.shape[position]) // (entries.shape[position] // blocks)).reshape((-1,) + (1,) * (entries.ndim - 1 - position))

    one_side = jax.random.permutation(key, blocks)[block_of(target)]
    far = (block_of(target) + blocks // 2) % blocks
    return jnp.where((block_of(source) == one_side) | (block_of(source) == far), factor * entries, entries)


def levels(key, shape, shards, smallest, top_value):
    def one(dim, shards_of):
        heights = jax.random.uniform(jax.random.fold_in(jax.random.fold_in(key, 6), dim), (shards_of,), jnp.float32, smallest / len(shards), top_value / len(shards))
        return jnp.repeat(jnp.exp(heights), shape[dim] // shards_of).reshape((-1,) + (1,) * (len(shape) - dim - 1))

    loudness = one(*shards[0])
    for cut in shards[1:]:
        loudness = loudness * one(*cut)
    return loudness


def noise(own_key, shape, width, reach, cuts=(), held_as=jnp.bfloat16):
    entries = width * jax.random.normal(own_key, shape, jnp.float32)
    if cuts:
        entries = entries * levels(own_key, shape, cuts, -0.22, 0.18)
    return jnp.clip(entries, -reach, reach).astype(held_as)


def noise_with(own_key, shape, deviation, reach, pieces, heavy, kind=jnp.bfloat16):
    values = deviation * jax.random.normal(own_key, shape, jnp.float32)
    if pieces:
        values = values * levels(own_key, shape, pieces, -0.22, 0.18)
    return jnp.clip(spiked(values, jax.random.fold_in(own_key, 3), *heavy), -reach, reach).astype(kind)


def setup_inputs(seed: int = 0) -> dict:
    arg_keys = jax.random.split(jax.random.key(seed), 17)
    return {
        "hidden_in": noise_with(arg_keys[0], (TOKENS, D), 1.0, 6.0, ((0, 8), (1, 4)), (0, 1, 8, 2.0)),
        "out_grad": noise_with(arg_keys[1], (TOKENS, D), 1.0, 6.0, ((0, 8), (1, 4)), (0, 1, 8, 2.0)),
        "norm_gain": jnp.clip(1.0 + 0.18 * jax.random.normal(arg_keys[2], (D,), jnp.float32), 0.1, 1.9),
        "gate_weight": noise(arg_keys[3], (D, D_INNER), D ** -0.5, 0.1875, ((1, 4),)),
        "value_weight": noise(arg_keys[4], (D, D_INNER), D ** -0.5, 0.1875, ((1, 4),)),
        "step_weight": noise(arg_keys[5], (D, HEADS), (D // 4) ** -0.5, 0.375, ((1, 4),)),
        "state_weight": noise(arg_keys[6], (D, 2 * STATE), D ** -0.5, 0.1875),
        "value_taps": noise(arg_keys[7], (CONV, D_INNER), 0.5, 3.0, ((1, 4),), jnp.float32),
        "value_bias": jnp.clip(jax.random.uniform(arg_keys[8], (D_INNER,), jnp.float32, -0.5, 0.5) * levels(arg_keys[8], (D_INNER,), ((0, 4),), -0.4, 0.0), -0.5, 0.5),
        "state_taps": noise(arg_keys[9], (CONV, 2 * STATE), 0.5, 3.0, (), jnp.float32),
        "state_bias": jnp.clip(jax.random.uniform(arg_keys[10], (2 * STATE,), jnp.float32, -0.5, 0.5), -0.5, 0.5),
        "step_bias": draw_step_bias(jax.random.fold_in(arg_keys[16], 71), 0),
        "decay_log": draw_decay_log(jax.random.fold_in(arg_keys[16], 71), 0),
        "skip_gain": jnp.clip(0.5 + 1.5 * jax.random.uniform(arg_keys[13], (HEADS,), jnp.float32) ** levels(arg_keys[13], (HEADS,), ((0, 4),), -0.2, 0.2), 0.5, 2.0),
        "gate_gain": jnp.clip(1.0 + 0.18 * jax.random.normal(arg_keys[14], (D_INNER,), jnp.float32), 0.1, 1.9),
        "out_weight": noise(arg_keys[15], (D_INNER, D), D_INNER ** -0.5, 0.125, ((0, 4),)),
    }


epsilon = 1e-05
highest = lax.Precision.HIGHEST

def rms_scale(source, gain):
    return source * lax.rsqrt(lax.optimization_barrier(jnp.mean(source * source, -1, keepdims=True)) + epsilon) * gain

def conv_mix(conv_in, taps, tap_bias):
    length = conv_in.shape[0]
    padded = jnp.concatenate([jnp.zeros((CONV - 1, conv_in.shape[1]), jnp.float32), conv_in], 0)
    conv_sum = tap_bias + taps[0] * padded[0:length]
    for offset in range(1, CONV):
        conv_sum = conv_sum + taps[offset] * padded[offset:offset + length]
    return jax.nn.silu(conv_sum)

def span_step(carry_state, block_data):
    values, key_rows, read_rows, log_decay, step_size = block_data
    cum_decay = jnp.cumsum(log_decay, axis=0).T
    index_rows = jnp.arange(SPAN)
    causal_mask = (index_rows[:, None] >= index_rows[None, :])[None, :, :]
    decay_table = jnp.exp(jnp.where(causal_mask, cum_decay[:, :, None] - cum_decay[:, None, :], -1e+30))
    scores = jnp.dot(read_rows, key_rows.T, precision=highest, preferred_element_type=jnp.float32)
    weights = scores[None, :, :] * decay_table * step_size.T[:, None, :]
    inside = jnp.einsum('hqs,shp->qhp', weights, values, precision=highest)
    carried = jnp.exp(cum_decay.T)[:, :, None] * jnp.einsum('qn,hpn->qhp', read_rows, carry_state, precision=highest)
    last_decay = cum_decay[:, -1]
    tail_weight = jnp.exp(last_decay[None, :] - cum_decay.T) * step_size
    new_state = jnp.exp(last_decay)[:, None, None] * carry_state + jnp.einsum('sh,shp,sn->hpn', tail_weight, values, key_rows, precision=highest)
    return (new_state, inside + carried)

def mixer(gate_in, conv_in, step_raw, value_taps, value_bias, state_taps, state_bias, step_bias, decay_log, skip_gain, gate_gain):
    taps = jnp.concatenate([value_taps, state_taps], 1)
    tap_bias = jnp.concatenate([value_bias, state_bias], 0)
    activated = conv_mix(conv_in, taps, tap_bias)
    length = activated.shape[0]
    values = activated[:, :D_INNER].reshape(length, HEADS, HEAD_DIM)
    key_rows = activated[:, D_INNER:D_INNER + STATE]
    read_rows = activated[:, D_INNER + STATE:]
    step_size = jax.nn.softplus(step_raw + step_bias)
    log_decay = -step_size * jnp.exp(decay_log)
    block_count = length // SPAN
    blocks = (values.reshape(block_count, SPAN, HEADS, HEAD_DIM), key_rows.reshape(block_count, SPAN, STATE), read_rows.reshape(block_count, SPAN, STATE), log_decay.reshape(block_count, SPAN, HEADS), step_size.reshape(block_count, SPAN, HEADS))
    start_state = jnp.zeros((HEADS, HEAD_DIM, STATE), jnp.float32)
    final_state, block_outs = lax.scan(jax.checkpoint(span_step), start_state, blocks)
    mixed_rows = block_outs.reshape(length, HEADS, HEAD_DIM) + skip_gain[:, None] * values
    gated_rows = mixed_rows.reshape(length, D_INNER) * jax.nn.silu(gate_in)
    gate_scale = lax.rsqrt(lax.optimization_barrier(jnp.mean(gated_rows * gated_rows, -1, keepdims=True)) + epsilon)
    return gated_rows * gate_scale * gate_gain

def reference(hidden_in, out_grad, norm_gain, gate_weight, value_weight, step_weight, state_weight, value_taps, value_bias, state_taps, state_bias, step_bias, decay_log, skip_gain, gate_gain, out_weight):
    source = hidden_in.astype(jnp.float32)
    normed_f, norm_back = jax.vjp(rms_scale, source, norm_gain)
    normed = normed_f.astype(jnp.bfloat16)
    gate_in = jnp.dot(normed, gate_weight, preferred_element_type=jnp.float32).astype(jnp.bfloat16)
    conv_value = jnp.dot(normed, value_weight, preferred_element_type=jnp.float32).astype(jnp.bfloat16)
    conv_shared = jnp.dot(normed, state_weight, preferred_element_type=jnp.float32).astype(jnp.bfloat16)
    step_raw = jnp.dot(normed, step_weight, preferred_element_type=jnp.float32).astype(jnp.bfloat16)
    conv_in = jnp.concatenate([conv_value, conv_shared], 1).astype(jnp.float32)
    normed_gate_f, mix_back = jax.vjp(mixer, gate_in.astype(jnp.float32), conv_in, step_raw.astype(jnp.float32), value_taps, value_bias, state_taps, state_bias, step_bias, decay_log, skip_gain, gate_gain)
    normed_gate = normed_gate_f.astype(jnp.bfloat16)
    block_out = (source + jnp.dot(normed_gate, out_weight, preferred_element_type=jnp.float32)).astype(jnp.bfloat16)
    grad_out_weight = jnp.dot(normed_gate.T, out_grad, preferred_element_type=jnp.float32)
    back_gate = jnp.dot(out_grad, out_weight.T, preferred_element_type=jnp.float32)
    grad_gate_in, grad_conv_in, grad_step_raw, grad_value_taps, grad_value_bias, grad_state_taps, grad_state_bias, grad_step_bias, grad_decay_log, grad_skip_gain, grad_gate_gain = mix_back(back_gate)
    gate_part = grad_gate_in.astype(jnp.bfloat16)
    value_part = grad_conv_in[:, :D_INNER].astype(jnp.bfloat16)
    shared_part = grad_conv_in[:, D_INNER:].astype(jnp.bfloat16)
    step_part = grad_step_raw.astype(jnp.bfloat16)
    grad_gate_weight = jnp.dot(normed.T, gate_part, preferred_element_type=jnp.float32)
    grad_value_weight = jnp.dot(normed.T, value_part, preferred_element_type=jnp.float32)
    grad_state_weight = jnp.dot(normed.T, shared_part, preferred_element_type=jnp.float32)
    grad_step_weight = jnp.dot(normed.T, step_part, preferred_element_type=jnp.float32)
    grad_normed = jnp.dot(gate_part, gate_weight.T, preferred_element_type=jnp.float32)
    grad_normed = grad_normed + jnp.dot(value_part, value_weight.T, preferred_element_type=jnp.float32)
    grad_normed = grad_normed + jnp.dot(shared_part, state_weight.T, preferred_element_type=jnp.float32)
    grad_normed = grad_normed + jnp.dot(step_part, step_weight.T, preferred_element_type=jnp.float32)
    grad_source, grad_norm_gain = norm_back(grad_normed)
    grad_in = (out_grad.astype(jnp.float32) + grad_source).astype(jnp.bfloat16)
    return (block_out, grad_in, grad_norm_gain, grad_gate_weight, grad_value_weight, grad_step_weight, grad_state_weight, grad_value_taps, grad_value_bias, grad_state_taps, grad_state_bias, grad_step_bias, grad_decay_log, grad_skip_gain, grad_gate_gain, grad_out_weight)
```

```python
import functools

import jax
import jax.numpy as jnp
from jax import lax
from jax.experimental import pallas as pl
from jax.experimental.pallas import tpu as pltpu
from jax.sharding import PartitionSpec as P

STATE = 128
CONV = 4
SPAN = 128
LANES = 128
WIDE = 256

BF = jnp.bfloat16
F32 = jnp.float32
epsilon = 1e-05


def dot(left, right, left_dim=1, right_dim=0):
    return lax.dot_general(
        left, right, (((left_dim,), (right_dim,)), ((), ())), preferred_element_type=F32
    )


def halves(value):
    upper = value.astype(BF)
    return upper, (value - upper.astype(F32)).astype(BF)


def dot_exact(value, picks, value_dim=1, picks_dim=0):
    first = value.astype(BF)
    rest = value - first.astype(F32)
    second = rest.astype(BF)
    third = (rest - second.astype(F32)).astype(BF)
    return (
        dot(first, picks, value_dim, picks_dim)
        + dot(second, picks, value_dim, picks_dim)
        + dot(third, picks, value_dim, picks_dim)
    )


def dot_pair(value, picks, value_dim=1, picks_dim=0):
    upper, lower = halves(value)
    return dot(upper, picks, value_dim, picks_dim) + dot(lower, picks, value_dim, picks_dim)


def softplus(value):
    small = jnp.exp(-jnp.abs(value))
    series = small * (1.0 - small * (0.5 - small * (1.0 / 3.0 - small * (0.25 - small * 0.2))))
    return jnp.maximum(value, 0.0) + jnp.where(small < 0.03, series, jnp.log(1.0 + small))


def whole(shape):
    return pl.BlockSpec(shape, lambda *_: (0,) * len(shape))


def call(body, grid, in_specs, out_specs, out_shape, scratch=(), flops=0, moved=0, name=None):
    spec = pltpu.PrefetchScalarGridSpec(
        num_scalar_prefetch=1,
        grid=grid,
        in_specs=in_specs,
        out_specs=out_specs,
        scratch_shapes=list(scratch),
    )
    return pl.pallas_call(
        body,
        grid_spec=spec,
        out_shape=out_shape,
        name=name,
        compiler_params=pltpu.CompilerParams(
            dimension_semantics=("arbitrary",) * len(grid), vmem_limit_bytes=56 * 2**20
        ),
        cost_estimate=pl.CostEstimate(flops=flops, transcendentals=0, bytes_accessed=moved),
    )


def shape_of(shape, dtype):
    return jax.ShapeDtypeStruct(shape, dtype)


def cyclic(value, axis, steps):
    count = lax.axis_size(axis)
    return lax.ppermute(value, axis, [(place, (place + steps) % count) for place in range(count)])


def swapped(value, axis, mask):
    count = lax.axis_size(axis)
    return lax.ppermute(value, axis, [(place, place ^ mask) for place in range(count)])


def neighbour(value, axis, steps):
    count = lax.axis_size(axis)
    first, last = (max(0, -steps), min(count, count - steps))
    return lax.ppermute(value, axis, [(place, place + steps) for place in range(first, last)])


def reversed_bits(count):
    bits = count.bit_length() - 1
    return [sum(((place >> bit) & 1) << (bits - 1 - bit) for bit in range(bits)) for place in range(count)]


def project_body(heads, scal, *refs):
    pieces = refs[:heads]
    gain, weights, normed, inv, gate, conv, step, tail = refs[heads:]
    width = pieces[0].shape[1]
    features = width * heads
    rows = [piece[...].astype(F32) for piece in pieces]
    total = sum(jnp.sum(row * row, 1, keepdims=True) for row in rows)
    scale = lax.rsqrt(total / features + epsilon)
    inv[...] = jnp.broadcast_to(scale, inv.shape)
    acc = None
    for shift in range(heads):
        start = pl.multiple_of(scal[heads + shift] * width, width)
        part = (rows[shift] * scale * gain[:, pl.ds(start, width)]).astype(BF)
        normed[:, pl.ds(start, width)] = part
        term = dot(part, weights[pl.ds(start, width), :])
        acc = term if acc is None else acc + term
    inner = gate.shape[1]
    mixed = conv.shape[1]
    gate[...] = acc[:, :inner].astype(BF)
    conv_rows = acc[:, inner : inner + mixed].astype(BF)
    conv[...] = conv_rows
    step[...] = acc[:, inner + mixed :].astype(BF)
    tail[...] = conv_rows[-16:]


def recur_body(scal, conv, before, step_raw, taps, bias, rows8, expand, lower, *refs):
    act, slope, step_out, cum_out, rows_out, adds, payload, ext, state, total = refs
    chunk = pl.program_id(0)
    span = conv.shape[0]
    inner = expand.shape[1]

    @pl.when(chunk == 0)
    def _():
        ext[0:8, :] = before[8:16, :].astype(F32)
        state[...] = jnp.zeros_like(state)
        total[...] = jnp.zeros_like(total)

    @pl.when(chunk > 0)
    def _():
        ext[0:8, :] = ext[span : span + 8, :]

    ext[8 : span + 8, :] = conv[...].astype(F32)
    conv_sum = bias[...]
    for offset in range(CONV):
        conv_sum = conv_sum + taps[offset : offset + 1, :] * ext[5 + offset : 5 + offset + span, :]
    sig = lax.logistic(conv_sum)
    active = conv_sum * sig
    act[...] = active
    slope[...] = sig * (1.0 + conv_sum * (1.0 - sig))
    step = softplus(step_raw[...].astype(F32) + rows8[0:1, :])
    log_decay = -step * jnp.exp(rows8[1:2, :])
    first = log_decay.astype(BF)
    rest = log_decay - first.astype(F32)
    second = rest.astype(BF)
    third = (rest - second.astype(F32)).astype(BF)
    cum = dot(lower[...], first) + dot(lower[...], second) + dot(lower[...], third)
    step_out[...] = step
    cum_out[...] = cum
    rows_out[0:8, :] = jnp.transpose(cum)[0:8, :]
    rows_out[8:16, :] = jnp.transpose(step)[0:8, :]
    last = cum[span - 1 : span, :]
    tail = jnp.exp(last - cum) * step
    tail_values = (active[:, :inner] * dot_pair(tail, expand[...])).astype(BF)
    keys = active[:, inner : inner + STATE].astype(BF)
    add = dot(keys, tail_values, 0, 0)
    adds[0] = add
    fade = dot_pair(jnp.broadcast_to(jnp.exp(last), (8, LANES)), expand[...])
    state[...] = state[...] * fade[0:1, :] + add
    total[...] = total[...] + jnp.broadcast_to(last, (8, LANES))

    @pl.when(chunk == pl.num_programs(0) - 1)
    def _():
        pack_state(payload, state[...], dot_exact(jnp.exp(total[...]), expand[...]))


def pack_state(payload, state, fade8):
    payload[0:STATE, :] = state.astype(BF)
    upper = fade8.astype(BF).astype(F32)
    payload[STATE : STATE + 16, :] = jnp.concatenate([upper, fade8 - upper], 0).astype(BF)


def join_body(first, last, scal, *refs):
    refs = list(refs)
    own, got = refs[0], refs[1]
    refs = refs[2:]
    flag = scal[0] > 0
    got_state = got[0:STATE, :].astype(F32)
    got_fade = got[STATE : STATE + 8, :].astype(F32) + got[STATE + 8 : STATE + 16, :].astype(F32)
    if first:
        zero = jnp.zeros_like(got_state)
        prefix = jnp.where(flag, got_state, zero)
        fade = jnp.where(flag, got_fade, jnp.ones_like(got_fade))
    else:
        old, old_fade = refs[0][...], refs[1][...]
        refs = refs[2:]
        prefix = jnp.where(flag, old_fade[0:1, :] * got_state + old, old)
        fade = jnp.where(flag, old_fade * got_fade, old_fade)
    refs[0][...] = prefix
    if not last:
        refs[1][...] = fade
        own_state = own[0:STATE, :].astype(F32)
        own_fade = own[STATE : STATE + 8, :].astype(F32) + own[STATE + 8 : STATE + 16, :].astype(F32)
        both = jnp.where(
            flag,
            own_fade[0:1, :] * got_state + own_state,
            got_fade[0:1, :] * own_state + got_state,
        )
        pack_state(refs[2], both, own_fade * got_fade)


def pair_terms(scores, mask, cum, rows, head):
    gap = cum[:, head : head + 1] - rows[head : head + 1, :]
    return jnp.exp(jnp.where(mask, gap, -1e30))


def inside_body(scal, act, cum, rows, skip, out):
    span = act.shape[0]
    inner = out.shape[1]
    keys = act[:, inner : inner + STATE].astype(BF)
    reads = act[:, inner + STATE :].astype(BF)
    scores = dot(reads, keys, 1, 1)
    query = lax.broadcasted_iota(jnp.int32, (span, span), 0)
    source = lax.broadcasted_iota(jnp.int32, (span, span), 1)
    mask = query >= source
    low = lax.broadcasted_iota(jnp.int32, (span, LANES), 1) < LANES // 2
    cum_now, rows_now = cum[...], rows[...]
    for pair in range(inner // LANES):
        block = slice(pair * LANES, (pair + 1) * LANES)
        values = act[:, block]
        acc = skip[:, block] * values
        for side in range(2):
            head = 2 * pair + side
            table = pair_terms(scores, mask, cum_now, rows_now, head)
            weights = (scores * table * rows_now[8 + head : 9 + head, :]).astype(BF)
            own = jnp.where(low if side == 0 else ~low, values, 0.0).astype(BF)
            acc = acc + dot(weights, own)
        out[:, block] = acc


def back_gate_body(heads, scal, *refs):
    pieces = refs[:heads]
    weight, full, out = refs[heads:]
    width = pieces[0].shape[1]
    acc = None
    for shift in range(heads):
        start = pl.multiple_of(scal[heads + shift] * width, width)
        piece = pieces[shift][...]
        full[:, pl.ds(start, width)] = piece
        term = dot(piece, weight[:, pl.ds(start, width)], 1, 1)
        acc = term if acc is None else acc + term
    out[...] = acc


def mix_body(scal, act, cum, local, adds, incoming, gate, back, gain, expand, *refs):
    mixed_out, states, sums, state = refs
    chunk = pl.program_id(0)
    span = act.shape[0]
    inner = local.shape[1]

    @pl.when(chunk == 0)
    def _():
        state[...] = incoming[...]

    now = state[...]
    states[0] = now
    reads = act[:, inner + STATE :].astype(BF)
    cum_now = cum[...]
    grown = dot_pair(jnp.exp(cum_now), expand[...])
    mixed = local[...] + grown * dot(reads, now.astype(BF))
    mixed_out[...] = mixed
    state[...] = now * grown[span - 1 : span, :] + adds[0]
    gate_now = gate[...].astype(F32)
    gated = mixed * gate_now * lax.logistic(gate_now)
    squares = jnp.sum(gated * gated, 1, keepdims=True)
    products = jnp.sum(gain[...] * back[...] * gated, 1, keepdims=True)
    lane = lax.broadcasted_iota(jnp.int32, (span, LANES), 1)
    both = jnp.where(lane == 0, squares, jnp.where(lane == 1, products, 0.0))
    sums[...] = jnp.transpose(both)[0:8, :]


def gated_back_body(heads, scal, *refs):
    totals = refs[:heads]
    act, cum, mixed, gate, back, gain, expand, weight = refs[heads : heads + 8]
    outs = refs[heads + 8 :]
    own_out, sent = outs[0], outs[1:heads]
    normed_gate, gate_part, grad_mixed, gain_grad, payload, state, total = outs[heads:]
    step = pl.program_id(0)
    span, inner = mixed.shape
    width = own_out.shape[1]

    @pl.when(step == 0)
    def _():
        state[...] = jnp.zeros_like(state)
        total[...] = jnp.zeros_like(total)
        gain_grad[...] = jnp.zeros_like(gain_grad)

    summed = sum(part[...] for part in totals)
    columns = jnp.transpose(jnp.concatenate([summed, jnp.zeros((LANES - 8, span), F32)], 0))
    inner_total = inner * heads
    scale = lax.rsqrt(columns[:, 0:1] / inner_total + epsilon)
    product = columns[:, 1:2]
    gate_now = gate[...].astype(F32)
    sig = lax.logistic(gate_now)
    silu = gate_now * sig
    mixed_now = mixed[...]
    gated = mixed_now * silu
    scaled = gated * scale
    rounded = (scaled * gain[...]).astype(BF)
    normed_gate[...] = rounded
    for shift in range(heads):
        start = pl.multiple_of(scal[shift] * width, width)
        term = dot(rounded, weight[:, pl.ds(start, width)])
        if shift == 0:
            own_out[...] = term
        else:
            sent[shift - 1][...] = term.astype(BF)
    back_now = back[...]
    gain_grad[...] = gain_grad[...] + jnp.broadcast_to(
        jnp.sum(back_now * scaled, 0, keepdims=True), gain_grad.shape
    )
    grad_gated = scale * (back_now * gain[...]) - gated * (
        scale * scale * scale * product * (1.0 / inner_total)
    )
    grad_now = grad_gated * silu
    grad_mixed[...] = grad_now
    gate_part[...] = (grad_gated * mixed_now * (sig * (1.0 + gate_now * (1.0 - sig)))).astype(BF)
    cum_now = cum[...]
    grown = dot_pair(jnp.exp(cum_now), expand[...])
    reads = act[:, inner + STATE :].astype(BF)
    state[...] = state[...] * grown[span - 1 : span, :] + dot(
        reads, (grown * grad_now).astype(BF), 0, 0
    )
    total[...] = total[...] + jnp.broadcast_to(cum_now[span - 1 : span, :], (8, LANES))

    @pl.when(step == pl.num_programs(0) - 1)
    def _():
        pack_state(payload, state[...], dot_exact(jnp.exp(total[...]), expand[...]))


def early_weights_body(count, scal, normed, grads, gate_part, normed_gate, keep, send):
    place = pl.program_id(0)
    inner = gate_part.shape[1]
    first = dot(normed[...], gate_part[...], 0, 0)
    second = dot(normed_gate[...], grads[...], 0, 0)

    def put(target):
        for block in range(inner // LANES):
            target[0, block * LANES : (block + 1) * LANES, :] = first[
                :, block * LANES : (block + 1) * LANES
            ].astype(BF)
        target[0, inner:, :] = second.astype(BF)

    pl.when(place < count // 2)(lambda: put(keep))
    pl.when(place >= count // 2)(lambda: put(send))


def late_weights_body(count, scal, normed, value_part, step_part, keep, send):
    place = pl.program_id(0)
    inner = value_part.shape[1]
    first = dot(normed[...], value_part[...], 0, 0)
    second = dot(step_part[...], normed[...], 0, 0)

    def put(target):
        for block in range(inner // LANES):
            target[0, block * LANES : (block + 1) * LANES, :] = first[
                :, block * LANES : (block + 1) * LANES
            ].astype(BF)
        target[0, inner:, :] = second[0:16, :].astype(BF)

    pl.when(place < count // 2)(lambda: put(keep))
    pl.when(place >= count // 2)(lambda: put(send))


def inside_back_body(scal, act, cum, rows, grad, values_out, maps_out, small_out):
    span = act.shape[0]
    inner = grad.shape[1]
    keys = act[:, inner : inner + STATE].astype(BF)
    reads = act[:, inner + STATE :].astype(BF)
    scores = dot(reads, keys, 1, 1)
    query = lax.broadcasted_iota(jnp.int32, (span, span), 0)
    source = lax.broadcasted_iota(jnp.int32, (span, span), 1)
    mask = query >= source
    lane = lax.broadcasted_iota(jnp.int32, (span, LANES), 1)
    low = lane < LANES // 2
    cum_now, rows_now = cum[...], rows[...]
    grad_scores = jnp.zeros((span, span), F32)
    from_rows = jnp.zeros((span, LANES), F32)
    step_rows = []
    for pair in range(inner // LANES):
        block = slice(pair * LANES, (pair + 1) * LANES)
        values = act[:, block].astype(BF)
        grads = grad[:, block]
        acc = None
        for side in range(2):
            head = 2 * pair + side
            step_row = rows_now[8 + head : 9 + head, :]
            own = jnp.where(low if side == 0 else ~low, grads, 0.0).astype(BF)
            grad_weights = dot(own, values, 1, 1)
            table = pair_terms(scores, mask, cum_now, rows_now, head)
            base = scores * table
            term = dot((base * step_row).astype(BF), own, 0, 0)
            acc = term if acc is None else acc + term
            flow = grad_weights * base
            step_rows.append(jnp.sum(flow, 0, keepdims=True))
            from_rows = from_rows + jnp.where(
                lane == head, jnp.sum(flow * step_row, 1, keepdims=True), 0.0
            )
            grad_scores = grad_scores + grad_weights * (table * step_row)
        values_out[:, block] = acc
    rounded = grad_scores.astype(BF)
    maps_out[:, :STATE] = dot(rounded, reads, 0, 0)
    maps_out[:, STATE:] = dot(rounded, keys)
    stacked = jnp.concatenate(step_rows, 0)
    empty = jnp.zeros((LANES - 8, span), F32)
    step_columns = jnp.transpose(jnp.concatenate([stacked, empty], 0))
    sum_columns = jnp.transpose(jnp.concatenate([stacked * rows_now[8:16, :], empty], 0))
    small_out[:, :LANES] = from_rows - sum_columns
    small_out[:, LANES:] = step_columns


def recur_back_body(scal, *refs):
    (
        act,
        slope,
        conv,
        conv_before,
        before,
        step_ref,
        cum_ref,
        step_raw,
        grad,
        values1,
        maps1,
        small1,
        states,
        outgoing,
        taps,
        rows8,
        skip,
        expand,
        lower,
        value_part,
        maps_part,
        step_part,
        last_rows,
        first_rows,
        tap_grads,
        small_grads,
        grad_state,
        after,
        ext,
    ) = refs
    place = pl.program_id(0)
    chunks = pl.num_programs(0)
    span, inner = grad.shape

    @pl.when(place == 0)
    def _():
        grad_state[...] = outgoing[...]
        after[span : span + 8, :] = jnp.zeros((8, after.shape[1]), F32)
        tap_grads[...] = jnp.zeros_like(tap_grads)
        small_grads[...] = jnp.zeros_like(small_grads)

    @pl.when(place > 0)
    def _():
        after[span : span + 8, :] = after[0:8, :]

    values = act[:, :inner]
    keys = act[:, inner : inner + STATE].astype(BF)
    reads = act[:, inner + STATE :].astype(BF)
    grad_now = grad[...]
    later = grad_state[...]
    later_bf = later.astype(BF)
    state = states[0]
    state_bf = state.astype(BF)
    cum = cum_ref[...]
    step = step_ref[...]
    last = cum[span - 1 : span, :]
    fading = jnp.exp(last - cum)
    tail = dot_pair(fading * step, expand[...])
    grown_small = jnp.exp(cum)
    grown = dot_pair(grown_small, expand[...])
    reach = dot(keys, later_bf)
    grad_values = values1[...] + tail * reach + skip[...] * grad_now
    grad_tail = dot_pair(values * reach, expand[...], 1, 1)
    grown_grad = grown * grad_now
    grown_bf = grown_grad.astype(BF)
    from_cum = dot_pair(grown_grad * dot(reads, state_bf), expand[...], 1, 1)
    grad_reads = maps1[:, STATE:] + dot(grown_bf, state_bf, 1, 1)
    grad_keys = maps1[:, :STATE] + dot((tail * values).astype(BF), later_bf, 1, 1)
    moved = step * fading * grad_tail
    kept = jnp.broadcast_to(jnp.sum(later * state, 0, keepdims=True), (8, inner))
    grad_last = jnp.sum(moved, 0, keepdims=True) + grown_small[
        span - 1 : span, :
    ] * dot_exact(kept, expand[...], 1, 1)[0:1, :]
    row = lax.broadcasted_iota(jnp.int32, (span, LANES), 0)
    grad_cum = small1[:, :LANES] + from_cum - moved + jnp.where(row == span - 1, grad_last, 0.0)
    first = grad_cum.astype(BF)
    rest = grad_cum - first.astype(F32)
    second = rest.astype(BF)
    third = (rest - second.astype(F32)).astype(BF)
    grad_log = dot(lower[...], first, 0, 0) + dot(lower[...], second, 0, 0) + dot(
        lower[...], third, 0, 0
    )
    strength = jnp.exp(rows8[1:2, :])
    grad_step = small1[:, LANES:] + fading * grad_tail - strength * grad_log
    grad_raw = grad_step * lax.logistic(step_raw[...].astype(F32) + rows8[0:1, :])
    lane = lax.broadcasted_iota(jnp.int32, (span, LANES), 1)
    step_part[...] = jnp.where(lane < inner // 64, grad_raw, 0.0).astype(BF)
    direct = dot_pair(
        jnp.broadcast_to(jnp.sum(grad_now * values, 0, keepdims=True), (8, inner)), expand[...], 1, 1
    )
    small_grads[0:1, :] = small_grads[0:1, :] + jnp.sum(grad_raw, 0, keepdims=True)
    small_grads[1:2, :] = small_grads[1:2, :] - strength * jnp.sum(
        grad_log * step, 0, keepdims=True
    )
    small_grads[2:3, :] = small_grads[2:3, :] + direct[0:1, :]

    after[0:span, :inner] = grad_values * slope[:, :inner]
    after[0:span, inner : inner + STATE] = grad_keys * slope[:, inner : inner + STATE]
    after[0:span, inner + STATE :] = grad_reads * slope[:, inner + STATE :]
    grad_sum = after[0:span, :]
    first_rows[...] = grad_sum[0:8, :]

    @pl.when(place == chunks - 1)
    def _():
        ext[0:8, :] = before[8:16, :].astype(F32)

    @pl.when(place < chunks - 1)
    def _():
        ext[0:8, :] = conv_before[8:16, :].astype(F32)

    ext[8 : span + 8, :] = conv[...].astype(F32)
    grad_conv = jnp.zeros_like(grad_sum)
    for offset in range(CONV):
        tap_grads[offset : offset + 1, :] = tap_grads[offset : offset + 1, :] + jnp.sum(
            grad_sum * ext[5 + offset : 5 + offset + span, :], 0, keepdims=True
        )
        grad_conv = grad_conv + taps[offset : offset + 1, :] * after[
            CONV - 1 - offset : CONV - 1 - offset + span, :
        ]
    tap_grads[CONV : CONV + 1, :] = tap_grads[CONV : CONV + 1, :] + jnp.sum(
        grad_sum, 0, keepdims=True
    )
    value_part[...] = grad_conv[:, :inner].astype(BF)
    maps_part[...] = grad_conv[:, inner:]

    @pl.when(place == 0)
    def _():
        last_rows[...] = grad_conv[span - 16 : span, :]

    grad_state[...] = later * grown[span - 1 : span, :] + dot(reads, grown_bf, 0, 0)


def rows_back_body(heads, scal, *refs):
    gate_part, value_part, step_part, maps_part, last_rows, ahead, taps, weights = refs[:8]
    outs = refs[8:]
    parts = outs[:heads]
    fixed, shifted = outs[heads:]
    place = pl.program_id(0)
    block = scal[place]
    rows, inner = value_part.shape
    features = weights.shape[0]
    fixed[...] = value_part[...]
    shifted[0:16, :] = jnp.zeros((16, shifted.shape[1]), F32)
    shifted[16:24, :] = ahead[...]
    corner = last_rows[...]
    for offset in range(CONV):
        corner = corner + taps[offset : offset + 1, :] * shifted[3 - offset : 19 - offset, :]
    at_end = block == heads - 1

    @pl.when(at_end)
    def _():
        fixed[rows - 16 : rows, :] = corner[:, :inner].astype(BF)

    maps = maps_part[...]
    maps_end = jnp.where(at_end, corner[:, inner:], maps[rows - 16 :, :])
    maps = jnp.concatenate([maps[: rows - 16, :], maps_end], 0)
    mixed = inner + taps.shape[1]
    total = dot(gate_part[...], weights[:, :inner], 1, 1)
    total = total + dot(fixed[...], weights[:, inner : 2 * inner], 1, 1)
    total = total + dot(step_part[...], weights[:, mixed:], 1, 1)
    for shift in range(heads):

        def put(target=parts[shift]):
            target[:, :features] = total.astype(target.dtype)
            target[:, features:] = maps.astype(target.dtype)

        pl.when(place == shift)(put)


def input_back_body(heads, scal, *refs):
    got = refs[:heads]
    pieces = refs[heads : 2 * heads]
    grads, inv, gain, state_weight, tap_grads = refs[2 * heads : 2 * heads + 5]
    outs = refs[2 * heads + 5 :]
    sent = outs[:heads]
    rows, features = grads.shape
    width = features // heads
    total = got[0][...].astype(F32)
    for part in got[1:]:
        total = total + part[...].astype(F32)
    shared = total[:, features:].astype(BF)
    grad_normed = total[:, :features] + dot(shared, state_weight[...], 1, 1)
    full = outs[heads]
    for shift in range(heads):
        start = pl.multiple_of(scal[heads + shift] * width, width)
        full[:, pl.ds(start, width)] = pieces[shift][...].astype(F32)
    scale = inv[:, 0:1]
    unit = full[...] * scale
    scaled = grad_normed * gain[...]
    mean = jnp.sum(scaled * unit, 1, keepdims=True) * (1.0 / features)
    gain_grad = jnp.sum(grad_normed * unit, 0, keepdims=True)
    full[...] = grads[...].astype(F32) + scale * (scaled - unit * mean)
    inner = tap_grads.shape[1] - 2 * STATE
    maps = tap_grads[:, inner:]
    small = jnp.concatenate(
        [
            jnp.concatenate([maps, jnp.zeros_like(maps)], 1),
            jnp.concatenate(
                [gain_grad[:, :512], gain_grad[:, 512:], jnp.zeros((6, 512), F32)], 0
            ),
        ],
        0,
    )
    upper = small.astype(BF)
    lower = (small - upper.astype(F32)).astype(BF)
    for shift in range(heads):
        start = pl.multiple_of(scal[shift] * width, width)
        target = sent[shift]
        target[0:rows, 0:width] = full[:, pl.ds(start, width)].astype(BF)
        target[0:rows, width:] = shared
        target[rows : rows + 16, :] = upper
        target[rows + 16 : rows + 32, :] = lower


def finish_body(heads, count, scal, *refs):
    got = refs[:heads]
    normed, grad_in, small = refs[heads : heads + 3]
    outs = refs[heads + 3 :]
    weights = outs[-1]
    rows = got[0].shape[0] - 32
    width = grad_in.shape[1]
    acc = None
    sums = None
    for shift in range(heads):
        start = pl.multiple_of(scal[heads + shift] * rows, rows)
        part = got[shift]
        grad_in[pl.ds(start, rows), :] = part[0:rows, 0:width]
        term = dot(normed[pl.ds(start, rows), :], part[0:rows, width:], 0, 0)
        acc = term if acc is None else acc + term
        extra = part[rows : rows + 16, :].astype(F32) + part[rows + 16 :, :].astype(F32)
        sums = extra if sums is None else sums + extra
    small[...] = sums
    weights[...] = acc
    if len(outs) == 1:
        return
    block = weights.shape[0] // count
    piece = block // heads
    for place in range(count):
        start = pl.multiple_of(scal[2 * heads + place] * block + scal[0] * piece, piece)
        value = weights[pl.ds(start, piece), :].astype(BF)
        outs[place // (count // 2)][place % (count // 2)] = value


def chain(payload, place, backward):
    count = lax.axis_size("seq")
    rows, width = payload.shape
    mask = 1
    prefix = None
    own = payload
    while mask < count:
        first, last = mask == 1, 2 * mask >= count
        got = swapped(own, "seq", mask)
        upper = (place & mask) // mask
        flag = (1 - upper if backward else upper).astype(jnp.int32).reshape(1)
        outs = [shape_of((STATE, width), F32)]
        if not last:
            outs += [shape_of((8, width), F32), shape_of((rows, width), BF)]
        args = [own, got] + ([] if first else list(prefix))
        made = call(
            functools.partial(join_body, first, last),
            (1,),
            [whole(arg.shape) for arg in args],
            [whole(out.shape) for out in outs],
            outs,
            moved=2**20,
            name="join",
        )(flag, *args)
        if last:
            return made[0]
        prefix, own = (made[0], made[1]), made[2]
        mask *= 2


def scatter_sum(keep, send):
    count = lax.axis_size("seq")
    mask = 1
    terms = [keep]
    while True:
        got = swapped(send, "seq", mask)
        terms.append(got)
        mask *= 2
        if mask >= count:
            break
        half = got.shape[0] // 2
        send = sum(term[half : 2 * half].astype(F32) for term in terms).astype(BF)
    return sum(term[0].astype(F32) for term in terms)


def total_sum(value, axis):
    count = lax.axis_size(axis)
    mask = 1
    while mask < count:
        value = value + swapped(value, axis, mask)
        mask *= 2
    return value


def per_device(
    hidden_in,
    out_grad,
    norm_gain,
    gate_weight,
    value_weight,
    step_weight,
    state_weight,
    value_taps,
    value_bias,
    state_taps,
    state_bias,
    step_bias,
    decay_log,
    skip_gain,
    gate_gain,
    out_weight,
):
    heads = lax.axis_size("head")
    count = lax.axis_size("seq")
    head_id = lax.axis_index("head")
    seq_id = lax.axis_index("seq")
    tokens, width = hidden_in.shape
    features = norm_gain.shape[0]
    inner = gate_weight.shape[1]
    local_heads = step_weight.shape[1]
    mixed = inner + 2 * STATE
    chunks = tokens // SPAN
    around = jnp.arange(heads, dtype=jnp.int32)
    order = seq_id.astype(jnp.int32) ^ jnp.asarray(reversed_bits(count), jnp.int32)
    scal = jnp.concatenate([(head_id + around) % heads, (head_id - around) % heads, order])
    scal = scal.astype(jnp.int32)

    weights = jnp.concatenate(
        [
            gate_weight,
            value_weight,
            state_weight,
            jnp.pad(step_weight, ((0, 0), (0, LANES - local_heads))),
        ],
        1,
    )
    taps = jnp.concatenate([value_taps, state_taps], 1)
    bias = jnp.concatenate([value_bias, state_bias])[None, :]
    lane_pad = ((0, 0), (0, LANES - local_heads))
    rows8 = jnp.pad(jnp.stack([step_bias, decay_log]), ((0, 6), (0, LANES - local_heads)))
    skip = jnp.repeat(skip_gain, inner // local_heads)[None, :]
    gain = norm_gain[None, :]
    out_gain = gate_gain[None, :]
    expand = (
        jnp.arange(LANES)[:, None] == (jnp.arange(inner) // (inner // local_heads))[None, :]
    ).astype(BF)
    lower = (jnp.arange(SPAN)[:, None] >= jnp.arange(SPAN)[None, :]).astype(BF)

    pieces = [hidden_in] + [cyclic(hidden_in, "head", k) for k in range(1, heads)]

    def rows_block(columns, size=SPAN):
        return pl.BlockSpec((size, columns), lambda i, s: (i, 0))

    def rows_back(columns, size=SPAN):
        return pl.BlockSpec((size, columns), lambda i, s: (chunks - 1 - i, 0))

    normed, inv, gate, conv, step_raw, tail = call(
        functools.partial(project_body, heads),
        (chunks,),
        [rows_block(width)] * heads + [whole(gain.shape), whole(weights.shape)],
        [
            rows_block(features),
            rows_block(LANES),
            rows_block(inner),
            rows_block(mixed),
            rows_block(LANES),
            whole((16, mixed)),
        ],
        [
            shape_of((tokens, features), BF),
            shape_of((tokens, LANES), F32),
            shape_of((tokens, inner), BF),
            shape_of((tokens, mixed), BF),
            shape_of((tokens, LANES), BF),
            shape_of((16, mixed), BF),
        ],
        flops=2 * tokens * features * weights.shape[1],
        moved=8 * 2**20,
        name="project",
    )(scal, *pieces, gain, weights)

    before = neighbour(tail, "seq", 1)

    act, slope, step, cum, rows, adds, payload = call(
        recur_body,
        (chunks,),
        [
            rows_block(mixed),
            whole((16, mixed)),
            rows_block(LANES),
            whole(taps.shape),
            whole(bias.shape),
            whole(rows8.shape),
            whole(expand.shape),
            whole(lower.shape),
        ],
        [
            rows_block(mixed),
            rows_block(mixed),
            rows_block(LANES),
            rows_block(LANES),
            pl.BlockSpec((16, SPAN), lambda i, s: (i, 0)),
            pl.BlockSpec((1, STATE, inner), lambda i, s: (i, 0, 0)),
            whole((STATE + 16, inner)),
        ],
        [
            shape_of((tokens, mixed), F32),
            shape_of((tokens, mixed), F32),
            shape_of((tokens, LANES), F32),
            shape_of((tokens, LANES), F32),
            shape_of((16 * chunks, SPAN), F32),
            shape_of((chunks, STATE, inner), F32),
            shape_of((STATE + 16, inner), BF),
        ],
        scratch=[
            pltpu.VMEM((SPAN + 8, mixed), F32),
            pltpu.VMEM((STATE, inner), F32),
            pltpu.VMEM((8, LANES), F32),
        ],
        flops=2 * tokens * STATE * inner,
        moved=8 * 2**20,
        name="recur",
    )(scal, conv, before, step_raw, taps, bias, rows8, expand, lower)

    incoming = chain(payload, seq_id, False)

    small_rows = pl.BlockSpec((16, SPAN), lambda i, s: (i, 0))
    (local,) = call(
        inside_body,
        (chunks,),
        [rows_block(mixed), rows_block(LANES), small_rows, whole(skip.shape)],
        [rows_block(inner)],
        [shape_of((tokens, inner), F32)],
        flops=2 * tokens * SPAN * inner,
        moved=8 * 2**20,
        name="inside",
    )(scal, act, cum, rows, skip)

    held, _ = lax.optimization_barrier((out_grad, pieces[-1]))
    grad_pieces = [out_grad] + [cyclic(held, "head", k) for k in range(1, heads)]
    grads, back = call(
        functools.partial(back_gate_body, heads),
        (chunks,),
        [rows_block(width)] * heads + [whole(out_weight.shape)],
        [rows_block(features), rows_block(inner)],
        [shape_of((tokens, features), BF), shape_of((tokens, inner), F32)],
        flops=2 * tokens * inner * features,
        moved=4 * 2**20,
        name="back_gate",
    )(scal, *grad_pieces, out_weight)

    chunk_state = pl.BlockSpec((1, STATE, inner), lambda i, s: (i, 0, 0))
    mixed_rows, states, sums = call(
        mix_body,
        (chunks,),
        [
            rows_block(mixed),
            rows_block(LANES),
            rows_block(inner),
            chunk_state,
            whole((STATE, inner)),
            rows_block(inner),
            rows_block(inner),
            whole(out_gain.shape),
            whole(expand.shape),
        ],
        [rows_block(inner), chunk_state, pl.BlockSpec((8, SPAN), lambda i, s: (0, i))],
        [
            shape_of((tokens, inner), F32),
            shape_of((chunks, STATE, inner), F32),
            shape_of((8, tokens), F32),
        ],
        scratch=[pltpu.VMEM((STATE, inner), F32)],
        flops=2 * tokens * STATE * inner,
        moved=8 * 2**20,
        name="mix",
    )(scal, act, cum, local, adds, incoming, gate, back, out_gain, expand)

    totals = [sums] + [cyclic(sums, "head", k) for k in range(1, heads)]

    sums_back = pl.BlockSpec((8, SPAN), lambda i, s: (0, chunks - 1 - i))
    made = call(
        functools.partial(gated_back_body, heads),
        (chunks,),
        [sums_back] * heads
        + [
            rows_back(mixed),
            rows_back(LANES),
            rows_back(inner),
            rows_back(inner),
            rows_back(inner),
            whole(out_gain.shape),
            whole(expand.shape),
            whole(out_weight.shape),
        ],
        [rows_back(width)] * heads
        + [
            rows_back(inner),
            rows_back(inner),
            rows_back(inner),
            whole((8, inner)),
            whole((STATE + 16, inner)),
        ],
        [shape_of((tokens, width), F32)]
        + [shape_of((tokens, width), BF)] * (heads - 1)
        + [
            shape_of((tokens, inner), BF),
            shape_of((tokens, inner), BF),
            shape_of((tokens, inner), F32),
            shape_of((8, inner), F32),
            shape_of((STATE + 16, inner), BF),
        ],
        scratch=[pltpu.VMEM((STATE, inner), F32), pltpu.VMEM((8, LANES), F32)],
        flops=2 * tokens * inner * features,
        moved=8 * 2**20,
        name="gated_back",
    )(scal, *totals, act, cum, mixed_rows, gate, back, out_gain, expand, out_weight)
    own_out, sent_out = made[0], made[1:heads]
    normed_gate, gate_part, grad_mixed, gain_grad, back_payload = made[heads:]

    outgoing = chain(back_payload, seq_id, True)

    out_terms = [cyclic(part, "head", k + 1) for k, part in enumerate(sent_out)]
    out_total = hidden_in.astype(F32) + own_out
    for part in out_terms:
        out_total = out_total + part.astype(F32)
    block_out = out_total.astype(BF)

    values1, maps1, small1 = call(
        inside_back_body,
        (chunks,),
        [rows_block(mixed), rows_block(LANES), small_rows, rows_block(inner)],
        [rows_block(inner), rows_block(2 * STATE), rows_block(2 * LANES)],
        [
            shape_of((tokens, inner), F32),
            shape_of((tokens, 2 * STATE), F32),
            shape_of((tokens, 2 * LANES), F32),
        ],
        flops=4 * tokens * SPAN * inner,
        moved=8 * 2**20,
        name="inside_back",
    )(scal, act, cum, rows, grad_mixed)

    groups = features // LANES
    paired = groups == count
    column_scal = scal if paired else jnp.concatenate([scal[: 2 * heads], jnp.arange(groups, dtype=jnp.int32)])
    half = groups // 2
    column_block = pl.BlockSpec((tokens, LANES), lambda i, s: (0, s[2 * heads + i]))

    def keep_block(size):
        return pl.BlockSpec((1, size, LANES), lambda i, s: (jnp.minimum(i, half - 1), 0, 0))

    def send_block(size):
        return pl.BlockSpec((1, size, LANES), lambda i, s: (jnp.maximum(i - half, 0), 0, 0))

    early_keep, early_send = call(
        functools.partial(early_weights_body, groups),
        (groups,),
        [column_block, column_block, whole((tokens, inner)), whole((tokens, inner))],
        [keep_block(2 * inner), send_block(2 * inner)],
        [shape_of((half, 2 * inner, LANES), BF)] * 2,
        flops=4 * tokens * inner * features,
        moved=6 * 2**20,
        name="early_weights",
    )(column_scal, normed, grads, gate_part, normed_gate)

    per_span = SPAN // 16
    back_state = pl.BlockSpec((1, STATE, inner), lambda i, s: (chunks - 1 - i, 0, 0))
    value_part, maps_part, step_part, last_rows, first_rows, tap_grads, small_grads = call(
        recur_back_body,
        (chunks,),
        [
            rows_back(mixed),
            rows_back(mixed),
            rows_back(mixed),
            pl.BlockSpec(
                (16, mixed), lambda i, s: (jnp.maximum((chunks - 1 - i) * per_span - 1, 0), 0)
            ),
            whole((16, mixed)),
            rows_back(LANES),
            rows_back(LANES),
            rows_back(LANES),
            rows_back(inner),
            rows_back(inner),
            rows_back(2 * STATE),
            rows_back(2 * LANES),
            back_state,
            whole((STATE, inner)),
            whole(taps.shape),
            whole(rows8.shape),
            whole(skip.shape),
            whole(expand.shape),
            whole(lower.shape),
        ],
        [
            rows_back(inner),
            rows_back(2 * STATE),
            rows_back(LANES),
            whole((16, mixed)),
            whole((8, mixed)),
            whole((8, mixed)),
            whole((8, LANES)),
        ],
        [
            shape_of((tokens, inner), BF),
            shape_of((tokens, 2 * STATE), F32),
            shape_of((tokens, LANES), BF),
            shape_of((16, mixed), F32),
            shape_of((8, mixed), F32),
            shape_of((8, mixed), F32),
            shape_of((8, LANES), F32),
        ],
        scratch=[
            pltpu.VMEM((STATE, inner), F32),
            pltpu.VMEM((SPAN + 8, mixed), F32),
            pltpu.VMEM((SPAN + 8, mixed), F32),
        ],
        flops=8 * tokens * STATE * inner,
        moved=16 * 2**20,
        name="recur_back",
    )(
        scal,
        act,
        slope,
        conv,
        conv,
        before,
        step,
        cum,
        step_raw,
        grad_mixed,
        values1,
        maps1,
        small1,
        states,
        outgoing,
        taps,
        rows8,
        skip,
        expand,
        lower,
    )

    ahead = neighbour(first_rows, "seq", -1)
    part_rows = tokens // heads

    def token_block(columns):
        return pl.BlockSpec((part_rows, columns), lambda i, s: (s[i], 0))

    packed = features + 2 * STATE
    made = call(
        functools.partial(rows_back_body, heads),
        (heads,),
        [
            token_block(inner),
            token_block(inner),
            token_block(LANES),
            token_block(2 * STATE),
            whole((16, mixed)),
            whole((8, mixed)),
            whole(taps.shape),
            whole(weights.shape),
        ],
        [whole((part_rows, packed))] * heads + [token_block(inner)],
        [shape_of((part_rows, packed), F32)]
        + [shape_of((part_rows, packed), BF)] * (heads - 1)
        + [shape_of((tokens, inner), BF)],
        scratch=[pltpu.VMEM((24, mixed), F32)],
        flops=2 * tokens * weights.shape[1] * features,
        moved=8 * 2**20,
        name="rows_back",
    )(scal, gate_part, value_part, step_part, maps_part, last_rows, ahead, taps, weights)
    fixed_part = made[heads]
    back_parts = [made[0]] + [cyclic(made[k], "head", k) for k in range(1, heads)]

    late_rows = inner + 16
    late_keep, late_send = call(
        functools.partial(late_weights_body, groups),
        (groups,),
        [column_block, whole((tokens, inner)), whole((tokens, LANES))],
        [keep_block(late_rows), send_block(late_rows)],
        [shape_of((half, late_rows, LANES), BF)] * 2,
        flops=2 * tokens * inner * features,
        moved=4 * 2**20,
        name="late_weights",
    )(column_scal, normed, fixed_part, step_part)

    own_rows = lambda columns: pl.BlockSpec((part_rows, columns), lambda i, s: (s[0], 0))
    final_parts = call(
        functools.partial(input_back_body, heads),
        (1,),
        [whole((part_rows, packed))] * heads
        + [own_rows(width)] * heads
        + [
            own_rows(features),
            own_rows(LANES),
            whole(gain.shape),
            whole(state_weight.shape),
            whole((8, mixed)),
        ],
        [whole((part_rows + 32, 2 * STATE + width))] * heads,
        [shape_of((part_rows + 32, 2 * STATE + width), BF)] * heads,
        scratch=[pltpu.VMEM((part_rows, features), F32)],
        flops=2 * tokens * features,
        moved=4 * 2**20,
        name="input_back",
    )(scal, *back_parts, *pieces, grads, inv, gain, state_weight, tap_grads)
    finals = [final_parts[0]] + [cyclic(final_parts[k], "head", k) for k in range(1, heads)]

    piece = features // count // heads
    half = count // 2
    blocked = paired and piece % 16 == 0
    shared_block = (half, piece, 2 * STATE)
    shared_outs = [(shared_block, BF)] * 2 if blocked else [((features, 2 * STATE), F32)]
    made = call(
        functools.partial(finish_body, heads, count),
        (1,),
        [whole((part_rows + 32, 2 * STATE + width))] * heads + [whole((tokens, features))],
        [whole((tokens, width)), whole((16, 512))] + [whole(shape) for shape, _ in shared_outs],
        [shape_of((tokens, width), BF), shape_of((16, 512), F32)]
        + [shape_of(*out) for out in shared_outs],
        scratch=[pltpu.VMEM((features, 2 * STATE), F32)] if blocked else [],
        flops=2 * tokens * features * 2 * STATE,
        moved=4 * 2**20,
        name="finish",
    )(scal, *finals, normed)
    grad_in, shared_small = made[:2]
    if blocked:
        grad_shared = scatter_sum(*made[2:])
    else:
        split = made[2].reshape(count, heads, piece, 2 * STATE)
        mine = lax.dynamic_index_in_dim(split, head_id, 1, keepdims=False)
        grad_shared = lax.psum_scatter(
            mine.reshape(-1, 2 * STATE), "seq", scatter_dimension=0, tiled=True
        )

    def unstacked(stack):
        blocks = stack.reshape(inner // LANES, -1, LANES)
        return blocks.transpose(1, 0, 2).reshape(blocks.shape[1], inner)

    if paired:
        early = scatter_sum(early_keep, early_send)
        late = scatter_sum(late_keep, late_send)
        grad_gate_weight = unstacked(early[:inner])
        grad_out_weight = early[inner:]
        grad_value_weight = unstacked(late[:inner])
        grad_step_weight = late[inner : inner + local_heads].T
    else:

        def joined(keep, send, first, last):
            stack = jnp.concatenate([keep, send])[:, first:last].astype(F32)
            return stack

        def as_rows(stack):
            return jnp.concatenate([unstacked(block) for block in stack], 0)

        def as_columns(stack):
            return jnp.concatenate(list(stack), 1)

        scatter = functools.partial(lax.psum_scatter, axis_name="seq", tiled=True)
        grad_gate_weight = scatter(
            as_rows(joined(early_keep, early_send, 0, inner)), scatter_dimension=0
        )
        grad_out_weight = scatter(
            as_columns(joined(early_keep, early_send, inner, 2 * inner)), scatter_dimension=1
        )
        grad_value_weight = scatter(
            as_rows(joined(late_keep, late_send, 0, inner)), scatter_dimension=0
        )
        grad_step_weight = scatter(
            as_columns(joined(late_keep, late_send, inner, inner + local_heads)).T,
            scatter_dimension=0,
        )

    small_pack = jnp.concatenate(
        [
            tap_grads[:, :inner],
            gain_grad[0:1],
            jnp.pad(small_grads[0:3].reshape(1, 3 * LANES), ((0, 0), (0, inner - 3 * LANES))),
            jnp.zeros((6, inner), F32),
            shared_small,
        ],
        0,
    )
    summed = total_sum(small_pack, "seq")
    scalars = summed[9]
    return (
        block_out,
        grad_in,
        summed[24:26].reshape(-1),
        grad_gate_weight,
        grad_value_weight,
        grad_step_weight,
        grad_shared,
        summed[0:CONV],
        summed[CONV],
        summed[16 : 16 + CONV, : 2 * STATE],
        summed[16 + CONV, : 2 * STATE],
        scalars[:local_heads],
        scalars[LANES : LANES + local_heads],
        scalars[2 * LANES : 2 * LANES + local_heads],
        summed[8],
        grad_out_weight,
    )


def solution(mesh):
    in_specs = (
        P("seq", "head"),
        P("seq", "head"),
        P(),
        P(None, "head"),
        P(None, "head"),
        P(None, "head"),
        P(),
        P(None, "head"),
        P("head"),
        P(),
        P(),
        P("head"),
        P("head"),
        P("head"),
        P("head"),
        P("head", None),
    )
    out_specs = (
        P("seq", "head"),
        P("seq", "head"),
        P(),
        P("seq", "head"),
        P("seq", "head"),
        P("seq", "head"),
        P(("seq", "head"), None),
        P(None, "head"),
        P("head"),
        P(),
        P(),
        P("head"),
        P("head"),
        P("head"),
        P("head"),
        P("head", "seq"),
    )
    return jax.shard_map(
        per_device, mesh=mesh, in_specs=in_specs, out_specs=out_specs, check_vma=False
    )
```

```python
import functools

import jax
import jax.numpy as jnp
from jax import lax
from jax.experimental import pallas as pl
from jax.experimental.pallas import tpu as pltpu
from jax.sharding import PartitionSpec as P


STATE = 128
CONV = 4
SPAN = 128
LANES = 128
VMEM_LIMIT = 14 * 2**20


BF = jnp.bfloat16
F32 = jnp.float32
epsilon = 1e-05


def dot(left, right, left_dim=1, right_dim=0):
    return lax.dot_general(
        left, right, (((left_dim,), (right_dim,)), ((), ())), preferred_element_type=F32
    )


def halves(value):
    upper = value.astype(BF)
    return upper, (value - upper.astype(F32)).astype(BF)


def dot_exact(value, picks, value_dim=1, picks_dim=0):
    first = value.astype(BF)
    rest = value - first.astype(F32)
    second = rest.astype(BF)
    third = (rest - second.astype(F32)).astype(BF)
    return (
        dot(first, picks, value_dim, picks_dim)
        + dot(second, picks, value_dim, picks_dim)
        + dot(third, picks, value_dim, picks_dim)
    )


def dot_pair(value, picks, value_dim=1, picks_dim=0):
    upper, lower = halves(value)
    return dot(upper, picks, value_dim, picks_dim) + dot(lower, picks, value_dim, picks_dim)


def softplus(value):
    small = jnp.exp(-jnp.abs(value))
    series = small * (1.0 - small * (0.5 - small * (1.0 / 3.0 - small * (0.25 - small * 0.2))))
    return jnp.maximum(value, 0.0) + jnp.where(small < 0.03, series, jnp.log(1.0 + small))


def whole(shape):
    return pl.BlockSpec(shape, lambda *_: (0,) * len(shape))


def resident(body, specs, scal, refs):
    views = []
    for spec, ref in zip(specs, refs):
        if spec is None or tuple(spec.block_shape) == tuple(ref.shape):
            views.append(ref)
            continue
        place = spec.index_map(pl.program_id(0), scal)
        window = []
        for index, size, full in zip(place, spec.block_shape, ref.shape):
            if size == full:
                window.append(slice(None))
            elif isinstance(index, int):
                window.append(pl.ds(index * size, size))
            else:
                window.append(pl.ds(pl.multiple_of(index * size, size), size))
        views.append(ref.at[tuple(window)])
    body(scal, *views)


def call(body, grid, in_specs, out_specs, out_shape, scratch=(), flops=0, moved=0, far=()):
    near = pl.BlockSpec(memory_space=pltpu.VMEM)
    specs = list(in_specs)
    specs += [None if place in far else spec for place, spec in enumerate(out_specs)]
    specs += [None] * len(scratch)

    def outer(scal, *refs):
        resident(body, specs, scal, refs)

    spec = pltpu.PrefetchScalarGridSpec(
        num_scalar_prefetch=1,
        grid=grid,
        in_specs=[near] * len(in_specs),
        out_specs=[spec if place in far else near for place, spec in enumerate(out_specs)],
        scratch_shapes=list(scratch),
    )
    made = pl.pallas_call(
        outer,
        grid_spec=spec,
        out_shape=[
            out if place in far else pltpu.VMEM(out.shape, out.dtype)
            for place, out in enumerate(out_shape)
        ],
        compiler_params=pltpu.CompilerParams(
            dimension_semantics=("arbitrary",) * len(grid), vmem_limit_bytes=VMEM_LIMIT
        ),
        cost_estimate=pl.CostEstimate(flops=flops, transcendentals=0, bytes_accessed=moved),
    )

    def run(scal, *args):
        return made(scal, *[pltpu.with_memory_space_constraint(arg, pltpu.VMEM) for arg in args])

    return run


def single(body, scal, args, outs, scratch=(), far=()):
    return call(
        body,
        (1,),
        [whole(arg.shape) for arg in args],
        [whole(out.shape) for out in outs],
        outs,
        scratch=scratch,
        moved=2**19,
        far=far,
    )(scal, *args)


def shape_of(shape, dtype):
    return jax.ShapeDtypeStruct(shape, dtype)


def cyclic(value, axis, steps):
    count = lax.axis_size(axis)
    return lax.ppermute(value, axis, [(place, (place + steps) % count) for place in range(count)])


def swapped(value, axis, mask):
    count = lax.axis_size(axis)
    return lax.ppermute(value, axis, [(place, place ^ mask) for place in range(count)])


def neighbour(value, axis, steps):
    count = lax.axis_size(axis)
    first, last = (max(0, -steps), min(count, count - steps))
    return lax.ppermute(value, axis, [(place, place + steps) for place in range(first, last)])


def reversed_bits(count):
    bits = count.bit_length() - 1
    return [sum(((place >> bit) & 1) << (bits - 1 - bit) for bit in range(bits)) for place in range(count)]


def project_body(heads, scal, *refs):
    pieces = refs[:heads]
    earlier = refs[heads : 2 * heads]
    gain, weights, normed, inv, gate, conv, step, before = refs[2 * heads :]
    width = pieces[0].shape[1]
    features = width * heads
    inner = gate.shape[1]
    mixed = conv.shape[1]

    def product(blocks, first, last, keep):
        rows = [block[...].astype(F32) for block in blocks]
        total = sum(jnp.sum(row * row, 1, keepdims=True) for row in rows)
        scale = lax.rsqrt(total / features + epsilon)
        acc = None
        for shift in range(heads):
            start = pl.multiple_of(scal[heads + shift] * width, width)
            part = (rows[shift] * scale * gain[:, pl.ds(start, width)]).astype(BF)
            if keep:
                normed[:, pl.ds(start, width)] = part
            term = dot(part, weights[pl.ds(start, width), first:last])
            acc = term if acc is None else acc + term
        return acc, scale

    acc, scale = product(pieces, 0, weights.shape[1], True)
    inv[...] = jnp.broadcast_to(scale, inv.shape)
    gate[...] = acc[:, :inner].astype(BF)
    conv[...] = acc[:, inner : inner + mixed].astype(BF)
    step[...] = acc[:, inner + mixed :].astype(BF)

    @pl.when(pl.program_id(0) == 0)
    def _():
        before[...] = product(earlier, inner, inner + mixed, False)[0].astype(BF)


def recur_body(scal, conv, before, step_raw, taps, bias, rows8, expand, lower, *refs):
    act, slope, step_out, cum_out, rows_out, adds, payload, ext, state, total = refs
    chunk = pl.program_id(0)
    span = conv.shape[0]
    inner = expand.shape[1]

    @pl.when(chunk == 0)
    def _():
        ext[0:8, :] = before[8:16, :].astype(F32)
        state[...] = jnp.zeros(state.shape, state.dtype)
        total[...] = jnp.zeros(total.shape, total.dtype)

    @pl.when(chunk > 0)
    def _():
        ext[0:8, :] = ext[span : span + 8, :]

    ext[8 : span + 8, :] = conv[...].astype(F32)
    conv_sum = bias[...]
    for offset in range(CONV):
        conv_sum = conv_sum + taps[offset : offset + 1, :] * ext[5 + offset : 5 + offset + span, :]
    sig = lax.logistic(conv_sum)
    active = conv_sum * sig
    act[...] = active
    slope[...] = sig * (1.0 + conv_sum * (1.0 - sig))
    step = softplus(step_raw[...].astype(F32) + rows8[0:1, :])
    log_decay = -step * jnp.exp(rows8[1:2, :])
    first = log_decay.astype(BF)
    rest = log_decay - first.astype(F32)
    second = rest.astype(BF)
    third = (rest - second.astype(F32)).astype(BF)
    cum = dot(lower[...], first) + dot(lower[...], second) + dot(lower[...], third)
    step_out[...] = step
    cum_out[...] = cum
    rows_out[0:8, :] = jnp.transpose(cum)[0:8, :]
    rows_out[8:16, :] = jnp.transpose(step)[0:8, :]
    last = cum[span - 1 : span, :]
    tail = jnp.exp(last - cum) * step
    tail_values = (active[:, :inner] * dot_pair(tail, expand[...])).astype(BF)
    keys = active[:, inner : inner + STATE].astype(BF)
    add = dot(keys, tail_values, 0, 0)
    adds[0] = add
    fade = dot_pair(jnp.broadcast_to(jnp.exp(last), (8, LANES)), expand[...])
    state[...] = state[...] * fade[0:1, :] + add
    total[...] = total[...] + jnp.broadcast_to(last, (8, LANES))

    @pl.when(chunk == pl.num_programs(0) - 1)
    def _():
        pack_state(payload, state[...], dot_exact(jnp.exp(total[...]), expand[...]))


def pack_state(payload, state, fade8):
    payload[0:STATE, :] = state.astype(BF)
    upper = fade8.astype(BF).astype(F32)
    payload[STATE : STATE + 16, :] = jnp.concatenate([upper, fade8 - upper], 0).astype(BF)


def join_body(first, last, mask, backward, scal, *refs):
    own, got = refs[:2]
    refs = refs[2:]
    upper = (scal[scal.shape[0] - 1] & mask) != 0
    flag = jnp.logical_not(upper) if backward else upper
    got_state = got[0:STATE, :].astype(F32)
    got_fade = got[STATE : STATE + 8, :].astype(F32) + got[STATE + 8 : STATE + 16, :].astype(F32)
    if first:
        prefix = jnp.where(flag, got_state, jnp.zeros(got_state.shape, F32))
        fade = jnp.where(flag, got_fade, jnp.ones(got_fade.shape, F32))
    else:
        old, old_fade = refs[0][...], refs[1][...]
        refs = refs[2:]
        prefix = jnp.where(flag, old_fade[0:1, :] * got_state + old, old)
        fade = jnp.where(flag, old_fade * got_fade, old_fade)
    refs[0][...] = prefix
    if last:
        return
    refs[1][...] = fade
    own_state = own[0:STATE, :].astype(F32)
    own_fade = own[STATE : STATE + 8, :].astype(F32) + own[STATE + 8 : STATE + 16, :].astype(F32)
    both = jnp.where(
        flag,
        own_fade[0:1, :] * got_state + own_state,
        got_fade[0:1, :] * own_state + got_state,
    )
    pack_state(refs[2], both, own_fade * got_fade)


def pair_terms(mask, cum, rows, head):
    gap = cum[:, head : head + 1] - rows[head : head + 1, :]
    return jnp.exp(jnp.where(mask, gap, -1e30))


def inside_body(scal, act, cum, rows, skip, out):
    span = act.shape[0]
    inner = out.shape[1]
    keys = act[:, inner : inner + STATE].astype(BF)
    reads = act[:, inner + STATE :].astype(BF)
    scores = dot(reads, keys, 1, 1)
    query = lax.broadcasted_iota(jnp.int32, (span, span), 0)
    source = lax.broadcasted_iota(jnp.int32, (span, span), 1)
    mask = query >= source
    low = lax.broadcasted_iota(jnp.int32, (span, LANES), 1) < LANES // 2
    cum_now, rows_now = cum[...], rows[...]
    for pair in range(inner // LANES):
        block = slice(pair * LANES, (pair + 1) * LANES)
        values = act[:, block]
        acc = skip[:, block] * values
        for side in range(2):
            head = 2 * pair + side
            table = pair_terms(mask, cum_now, rows_now, head)
            weights = (scores * table * rows_now[8 + head : 9 + head, :]).astype(BF)
            own = jnp.where(low if side == 0 else ~low, values, 0.0).astype(BF)
            acc = acc + dot(weights, own)
        out[:, block] = acc


def back_gate_body(heads, scal, *refs):
    pieces = refs[:heads]
    weight, full, out = refs[heads:]
    width = pieces[0].shape[1]
    acc = None
    for shift in range(heads):
        start = pl.multiple_of(scal[heads + shift] * width, width)
        piece = pieces[shift][...]
        full[:, pl.ds(start, width)] = piece
        term = dot(piece, weight[:, pl.ds(start, width)], 1, 1)
        acc = term if acc is None else acc + term
    out[...] = acc


def mix_body(scal, act, cum, local, adds, incoming, gate, back, gain, expand, *refs):
    mixed_out, states, sums, state = refs
    chunk = pl.program_id(0)
    span = act.shape[0]
    inner = local.shape[1]

    @pl.when(chunk == 0)
    def _():
        state[...] = incoming[...]

    now = state[...]
    states[0] = now
    reads = act[:, inner + STATE :].astype(BF)
    cum_now = cum[...]
    grown = dot_pair(jnp.exp(cum_now), expand[...])
    mixed = local[...] + grown * dot(reads, now.astype(BF))
    mixed_out[...] = mixed
    state[...] = now * grown[span - 1 : span, :] + adds[0]
    gate_now = gate[...].astype(F32)
    gated = mixed * gate_now * lax.logistic(gate_now)
    squares = jnp.sum(gated * gated, 1, keepdims=True)
    products = jnp.sum(gain[...] * back[...] * gated, 1, keepdims=True)
    lane = lax.broadcasted_iota(jnp.int32, (span, LANES), 1)
    both = jnp.where(lane == 0, squares, jnp.where(lane == 1, products, 0.0))
    sums[...] = jnp.transpose(both)[0:8, :]


def gated_back_body(heads, scal, *refs):
    totals = refs[:heads]
    act, cum, mixed, gate, back, gain, expand, weight = refs[heads : heads + 8]
    outs = refs[heads + 8 :]
    own_out, sent = outs[0], outs[1:heads]
    normed_gate, gate_part, grad_mixed, gain_grad, payload, state, total = outs[heads:]
    step = pl.program_id(0)
    span, inner = mixed.shape
    width = own_out.shape[1]

    @pl.when(step == 0)
    def _():
        state[...] = jnp.zeros(state.shape, state.dtype)
        total[...] = jnp.zeros(total.shape, total.dtype)
        gain_grad[...] = jnp.zeros(gain_grad.shape, gain_grad.dtype)

    summed = sum(part[...] for part in totals)
    columns = jnp.transpose(jnp.concatenate([summed, jnp.zeros((LANES - 8, span), F32)], 0))
    inner_total = inner * heads
    scale = lax.rsqrt(columns[:, 0:1] / inner_total + epsilon)
    product = columns[:, 1:2]
    gate_now = gate[...].astype(F32)
    sig = lax.logistic(gate_now)
    silu = gate_now * sig
    mixed_now = mixed[...]
    gated = mixed_now * silu
    scaled = gated * scale
    rounded = (scaled * gain[...]).astype(BF)
    normed_gate[...] = rounded
    for shift in range(heads):
        start = pl.multiple_of(scal[shift] * width, width)
        term = dot(rounded, weight[:, pl.ds(start, width)])
        if shift == 0:
            own_out[...] = term
        else:
            sent[shift - 1][...] = term.astype(BF)
    back_now = back[...]
    gain_grad[...] = gain_grad[...] + jnp.broadcast_to(
        jnp.sum(back_now * scaled, 0, keepdims=True), gain_grad.shape
    )
    grad_gated = scale * (back_now * gain[...]) - gated * (
        scale * scale * scale * product * (1.0 / inner_total)
    )
    grad_now = grad_gated * silu
    grad_mixed[...] = grad_now
    gate_part[...] = (grad_gated * mixed_now * (sig * (1.0 + gate_now * (1.0 - sig)))).astype(BF)
    cum_now = cum[...]
    grown = dot_pair(jnp.exp(cum_now), expand[...])
    reads = act[:, inner + STATE :].astype(BF)
    state[...] = state[...] * grown[span - 1 : span, :] + dot(
        reads, (grown * grad_now).astype(BF), 0, 0
    )
    total[...] = total[...] + jnp.broadcast_to(cum_now[span - 1 : span, :], (8, LANES))

    @pl.when(step == pl.num_programs(0) - 1)
    def _():
        pack_state(payload, state[...], dot_exact(jnp.exp(total[...]), expand[...]))


def cut_columns(heads, count, scal, full, keep, send):
    for place in range(count):
        start = pl.multiple_of(scal[2 * heads + place] * LANES, LANES)
        target = keep if place < count // 2 else send
        target[place % (count // 2)] = full[:, pl.ds(start, LANES)].astype(BF)


def early_body(heads, count, scal, gate_part, normed, normed_gate, grads, keep, send, full):
    inner = gate_part.shape[1]
    full[:inner, :] = dot(gate_part[...], normed[...], 0, 0)
    full[inner:, :] = dot(normed_gate[...], grads[...], 0, 0)
    cut_columns(heads, count, scal, full, keep, send)


def late_body(heads, count, scal, *refs):
    value_part, step_part, maps_part, last_rows, ahead, taps, normed = refs[:7]
    keep, send, fixed, maps_out, full, shifted = refs[7:]
    tokens, inner = value_part.shape
    shifted[0:16, :] = jnp.zeros((16, shifted.shape[1]), F32)
    shifted[16:24, :] = ahead[...]
    corner = last_rows[...]
    for offset in range(CONV):
        corner = corner + taps[offset : offset + 1, :] * shifted[3 - offset : 19 - offset, :]
    fixed[0 : tokens - 16, :] = value_part[0 : tokens - 16, :]
    fixed[tokens - 16 : tokens, :] = corner[:, :inner].astype(BF)
    maps_out[0 : tokens - 16, :] = maps_part[0 : tokens - 16, :].astype(BF)
    maps_out[tokens - 16 : tokens, :] = corner[:, inner:].astype(BF)
    rows = normed[...]
    maps = 2 * STATE
    full[:inner, :] = dot(fixed[...], rows, 0, 0)
    full[inner : inner + maps, :] = dot(maps_out[...], rows, 0, 0)
    full[inner + maps :, :] = dot(step_part[...], rows, 0, 0)[0:16, :]
    cut_columns(heads, count, scal, full, keep, send)


def inside_back_body(scal, act, cum, rows, grad, values_out, maps_out, small_out):
    span = act.shape[0]
    inner = grad.shape[1]
    keys = act[:, inner : inner + STATE].astype(BF)
    reads = act[:, inner + STATE :].astype(BF)
    scores = dot(reads, keys, 1, 1)
    query = lax.broadcasted_iota(jnp.int32, (span, span), 0)
    source = lax.broadcasted_iota(jnp.int32, (span, span), 1)
    mask = query >= source
    lane = lax.broadcasted_iota(jnp.int32, (span, LANES), 1)
    low = lane < LANES // 2
    cum_now, rows_now = cum[...], rows[...]
    grad_scores = jnp.zeros((span, span), F32)
    from_rows = jnp.zeros((span, LANES), F32)
    step_rows = []
    for pair in range(inner // LANES):
        block = slice(pair * LANES, (pair + 1) * LANES)
        values = act[:, block].astype(BF)
        grads = grad[:, block]
        acc = None
        for side in range(2):
            head = 2 * pair + side
            step_row = rows_now[8 + head : 9 + head, :]
            own = jnp.where(low if side == 0 else ~low, grads, 0.0).astype(BF)
            grad_weights = dot(own, values, 1, 1)
            table = pair_terms(mask, cum_now, rows_now, head)
            base = scores * table
            term = dot((base * step_row).astype(BF), own, 0, 0)
            acc = term if acc is None else acc + term
            flow = grad_weights * base
            step_rows.append(jnp.sum(flow, 0, keepdims=True))
            from_rows = from_rows + jnp.where(
                lane == head, jnp.sum(flow * step_row, 1, keepdims=True), 0.0
            )
            grad_scores = grad_scores + grad_weights * (table * step_row)
        values_out[:, block] = acc
    rounded = grad_scores.astype(BF)
    maps_out[:, :STATE] = dot(rounded, reads, 0, 0)
    maps_out[:, STATE:] = dot(rounded, keys)
    stacked = jnp.concatenate(step_rows, 0)
    empty = jnp.zeros((LANES - 8, span), F32)
    step_columns = jnp.transpose(jnp.concatenate([stacked, empty], 0))
    sum_columns = jnp.transpose(jnp.concatenate([stacked * rows_now[8:16, :], empty], 0))
    small_out[:, :LANES] = from_rows - sum_columns
    small_out[:, LANES:] = step_columns


def recur_back_body(scal, *refs):
    (
        act,
        slope,
        conv,
        conv_before,
        before,
        step_ref,
        cum_ref,
        step_raw,
        grad,
        values1,
        maps1,
        small1,
        states,
        outgoing,
        taps,
        rows8,
        skip,
        expand,
        lower,
        value_part,
        maps_part,
        step_part,
        last_rows,
        first_rows,
        tap_grads,
        small_grads,
        grad_state,
        after,
        ext,
    ) = refs
    place = pl.program_id(0)
    chunks = pl.num_programs(0)
    span, inner = grad.shape

    @pl.when(place == 0)
    def _():
        grad_state[...] = outgoing[...]
        after[span : span + 8, :] = jnp.zeros((8, after.shape[1]), F32)
        tap_grads[...] = jnp.zeros(tap_grads.shape, tap_grads.dtype)
        small_grads[...] = jnp.zeros(small_grads.shape, small_grads.dtype)

    @pl.when(place > 0)
    def _():
        after[span : span + 8, :] = after[0:8, :]

    values = act[:, :inner]
    keys = act[:, inner : inner + STATE].astype(BF)
    reads = act[:, inner + STATE :].astype(BF)
    grad_now = grad[...]
    later = grad_state[...]
    later_bf = later.astype(BF)
    state = states[0]
    state_bf = state.astype(BF)
    cum = cum_ref[...]
    step = step_ref[...]
    last = cum[span - 1 : span, :]
    fading = jnp.exp(last - cum)
    tail = dot_pair(fading * step, expand[...])
    grown_small = jnp.exp(cum)
    grown = dot_pair(grown_small, expand[...])
    reach = dot(keys, later_bf)
    grad_values = values1[...] + tail * reach + skip[...] * grad_now
    grad_tail = dot_pair(values * reach, expand[...], 1, 1)
    grown_grad = grown * grad_now
    grown_bf = grown_grad.astype(BF)
    from_cum = dot_pair(grown_grad * dot(reads, state_bf), expand[...], 1, 1)
    grad_reads = maps1[:, STATE:] + dot(grown_bf, state_bf, 1, 1)
    grad_keys = maps1[:, :STATE] + dot((tail * values).astype(BF), later_bf, 1, 1)
    moved = step * fading * grad_tail
    kept = jnp.broadcast_to(jnp.sum(later * state, 0, keepdims=True), (8, inner))
    grad_last = jnp.sum(moved, 0, keepdims=True) + grown_small[
        span - 1 : span, :
    ] * dot_exact(kept, expand[...], 1, 1)[0:1, :]
    row = lax.broadcasted_iota(jnp.int32, (span, LANES), 0)
    grad_cum = small1[:, :LANES] + from_cum - moved + jnp.where(row == span - 1, grad_last, 0.0)
    first = grad_cum.astype(BF)
    rest = grad_cum - first.astype(F32)
    second = rest.astype(BF)
    third = (rest - second.astype(F32)).astype(BF)
    grad_log = dot(lower[...], first, 0, 0) + dot(lower[...], second, 0, 0) + dot(
        lower[...], third, 0, 0
    )
    strength = jnp.exp(rows8[1:2, :])
    grad_step = small1[:, LANES:] + fading * grad_tail - strength * grad_log
    grad_raw = grad_step * lax.logistic(step_raw[...].astype(F32) + rows8[0:1, :])
    lane = lax.broadcasted_iota(jnp.int32, (span, LANES), 1)
    step_part[...] = jnp.where(lane < inner // 64, grad_raw, 0.0).astype(BF)
    direct = dot_pair(
        jnp.broadcast_to(jnp.sum(grad_now * values, 0, keepdims=True), (8, inner)), expand[...], 1, 1
    )
    small_grads[0:1, :] = small_grads[0:1, :] + jnp.sum(grad_raw, 0, keepdims=True)
    small_grads[1:2, :] = small_grads[1:2, :] - strength * jnp.sum(
        grad_log * step, 0, keepdims=True
    )
    small_grads[2:3, :] = small_grads[2:3, :] + direct[0:1, :]

    after[0:span, :inner] = grad_values * slope[:, :inner]
    after[0:span, inner : inner + STATE] = grad_keys * slope[:, inner : inner + STATE]
    after[0:span, inner + STATE :] = grad_reads * slope[:, inner + STATE :]
    grad_sum = after[0:span, :]
    first_rows[...] = grad_sum[0:8, :]

    @pl.when(place == chunks - 1)
    def _():
        ext[0:8, :] = before[8:16, :].astype(F32)

    @pl.when(place < chunks - 1)
    def _():
        ext[0:8, :] = conv_before[8:16, :].astype(F32)

    ext[8 : span + 8, :] = conv[...].astype(F32)
    grad_conv = jnp.zeros(grad_sum.shape, grad_sum.dtype)
    for offset in range(CONV):
        tap_grads[offset : offset + 1, :] = tap_grads[offset : offset + 1, :] + jnp.sum(
            grad_sum * ext[5 + offset : 5 + offset + span, :], 0, keepdims=True
        )
        grad_conv = grad_conv + taps[offset : offset + 1, :] * after[
            CONV - 1 - offset : CONV - 1 - offset + span, :
        ]
    tap_grads[CONV : CONV + 1, :] = tap_grads[CONV : CONV + 1, :] + jnp.sum(
        grad_sum, 0, keepdims=True
    )
    value_part[...] = grad_conv[:, :inner].astype(BF)
    maps_part[...] = grad_conv[:, inner:]

    @pl.when(place == 0)
    def _():
        last_rows[...] = grad_conv[span - 16 : span, :]

    grad_state[...] = later * grown[span - 1 : span, :] + dot(reads, grown_bf, 0, 0)


def rows_back_body(heads, scal, *refs):
    gate_part, value_part, step_part, maps_part, weights, inv = refs[:6]
    pieces = refs[6 : 6 + heads]
    outs = refs[6 + heads :]
    parts = outs[:heads]
    gain_grad, total, flow = outs[heads:]
    tokens, inner = value_part.shape
    features = weights.shape[0]
    width = features // heads
    rows = tokens // heads
    mixed = 2 * inner + 2 * STATE
    product = dot(gate_part[...], weights[:, :inner], 1, 1)
    product = product + dot(value_part[...], weights[:, inner : 2 * inner], 1, 1)
    product = product + dot(step_part[...], weights[:, mixed:], 1, 1)
    total[...] = product
    flow[...] = (product + dot(maps_part[...], weights[:, 2 * inner : mixed], 1, 1)) * inv[:, 0:1]
    for shift in range(heads):
        columns = pl.ds(pl.multiple_of(scal[heads + shift] * width, width), width)
        share = jnp.sum(flow[:, columns] * pieces[shift][...].astype(F32), 0, keepdims=True)
        gain_grad[:, columns] = jnp.broadcast_to(share, (8, width))
        block = pl.ds(pl.multiple_of(scal[shift] * rows, rows), rows)
        target = parts[shift]
        target[:, :features] = total[block, :].astype(target.dtype)
        target[:, features:] = maps_part[block, :].astype(target.dtype)


def input_back_body(heads, blocked, scal, *refs):
    got = refs[:heads]
    pieces = refs[heads : 2 * heads]
    grads, inv, gain, state_weight, small = refs[2 * heads : 2 * heads + 5]
    refs = refs[2 * heads + 5 :]
    if blocked:
        late, refs = refs[0], refs[1:]
    sent = refs[:heads]
    taps_out, rest_out, full = refs[heads:]
    rows, features = grads.shape
    width = features // heads
    total = got[0][...].astype(F32)
    for part in got[1:]:
        total = total + part[...].astype(F32)
    shared = total[:, features:].astype(BF)
    grad_normed = total[:, :features] + dot(shared, state_weight[...], 1, 1)
    for shift in range(heads):
        start = pl.multiple_of(scal[heads + shift] * width, width)
        full[:, pl.ds(start, width)] = pieces[shift][...].astype(F32)
    scale = inv[:, 0:1]
    unit = full[...] * scale
    scaled = grad_normed * gain[...]
    mean = jnp.sum(scaled * unit, 1, keepdims=True) * (1.0 / features)
    full[...] = grads[...].astype(F32) + scale * (scaled - unit * mean)
    lanes = small.shape[1]
    per = taps_out.shape[1] // lanes
    for row in range(CONV + 2):
        target = taps_out if row < CONV else rest_out
        place = row if row < CONV else row - CONV
        for part in range(per):
            target[place : place + 1, part * lanes : (part + 1) * lanes] = small[
                row * per + part : row * per + part + 1, :
            ]
    start = (CONV + 2) * per
    rest_out[2:5, 0:lanes] = small[start : start + 3, :]
    upper, lower = halves(small[start + 4 : start + 20, :])
    if blocked:
        piece = late.shape[0] // heads
    for shift in range(heads):
        start = pl.multiple_of(scal[shift] * width, width)
        target = sent[shift]
        target[0:rows, :] = full[:, pl.ds(start, width)].astype(BF)
        target[rows : rows + 16, :] = upper
        target[rows + 16 : rows + 32, :] = lower
        if blocked:
            first = pl.multiple_of(scal[shift] * piece, piece)
            high, low = halves(late[pl.ds(first, piece), :])
            target[rows + 32 : rows + 32 + piece, :] = high
            target[rows + 32 + piece : rows + 32 + 2 * piece, :] = low


def finish_body(heads, scal, *refs):
    got = refs[:heads]
    grad_in, small = refs[heads : heads + 2]
    outs = refs[heads + 2 :]
    rows = grad_in.shape[0] // heads
    sums, shared = None, None
    for shift in range(heads):
        start = pl.multiple_of(scal[heads + shift] * rows, rows)
        part = got[shift]
        grad_in[pl.ds(start, rows), :] = part[0:rows, :]
        extra = part[rows : rows + 16, :].astype(F32) + part[rows + 16 : rows + 32, :].astype(F32)
        sums = extra if sums is None else sums + extra
        if outs:
            piece = outs[0].shape[0]
            block = part[rows + 32 : rows + 32 + piece, :].astype(F32) + part[
                rows + 32 + piece : rows + 32 + 2 * piece, :
            ].astype(F32)
            shared = block if shared is None else shared + block
    small[...] = sums
    if outs:
        outs[0][...] = shared


def chain(payload, scal, backward):
    count = lax.axis_size("seq")
    rows, width = payload.shape
    mask = 1
    own, prefix = payload, ()
    while mask < count:
        got = swapped(own, "seq", mask)
        first, last = mask == 1, 2 * mask >= count
        outs = [shape_of((STATE, width), F32)]
        if not last:
            outs += [shape_of((8, width), F32), shape_of((rows, width), BF)]
        made = single(
            functools.partial(join_body, first, last, mask, backward),
            scal,
            [own, got, *prefix],
            outs,
        )
        if last:
            return made[0]
        prefix, own = (made[0], made[1]), made[2]
        mask = 2 * mask


def part_sum_body(half, scal, *refs):
    total = refs[0][half : 2 * half].astype(F32)
    for ref in refs[1:-1]:
        total = total + ref[half : 2 * half].astype(F32)
    refs[-1][...] = total.astype(BF)


def scatter_terms(keep, send, scal):
    count = lax.axis_size("seq")
    mask = 1
    terms = [keep]
    while True:
        got = swapped(send, "seq", mask)
        terms.append(got)
        mask *= 2
        if mask >= count:
            return terms
        half = got.shape[0] // 2
        (send,) = single(
            functools.partial(part_sum_body, half),
            scal,
            terms,
            [shape_of((half,) + keep.shape[1:], BF)],
        )


def early_end_body(scal, *refs):
    terms, (gate_out, weight_out) = refs[:-2], refs[-2:]
    total = terms[0][0].astype(F32)
    for term in terms[1:]:
        total = total + term[0].astype(F32)
    inner = weight_out.shape[0]
    gate_out[...] = jnp.transpose(total[:inner])
    weight_out[...] = total[inner:]


def late_end_body(scal, *refs):
    terms, (value_out, step_out, maps_out) = refs[:-3], refs[-3:]
    total = terms[0][0].astype(F32)
    for term in terms[1:]:
        total = total + term[0].astype(F32)
    inner = value_out.shape[1]
    maps = 2 * STATE
    value_out[...] = jnp.transpose(total[:inner])
    maps_out[...] = jnp.transpose(total[inner : inner + maps])
    steps = jnp.concatenate([total[inner + maps :], jnp.zeros((LANES - 16, LANES), F32)], 0)
    step_out[...] = jnp.transpose(steps)


def add_body(scal, left, right, out):
    out[...] = left[...] + right[...]


def total_sum(value, axis, scal):
    count = lax.axis_size(axis)
    mask = 1
    while mask < count:
        got = swapped(value, axis, mask)
        (value,) = single(add_body, scal, [value, got], [shape_of(value.shape, F32)])
        mask = mask * 2
    return value


def pack_body(scal, taps, gain, small, norm, out):
    inner = gain.shape[1]
    lanes = out.shape[1]
    maps = taps.shape[1] - inner
    out[...] = jnp.zeros(out.shape, F32)
    per = inner // lanes
    for row in range(CONV + 2):
        for part in range(per):
            place = slice(part * lanes, (part + 1) * lanes)
            source = gain[0:1, place] if row > CONV else taps[row : row + 1, place]
            out[row * per + part : row * per + part + 1, :] = source
    start = (CONV + 2) * per
    out[start : start + 3, 0:LANES] = small[0:3, :]
    out[start + 4 : start + 5 + CONV, 0:maps] = taps[0 : CONV + 1, inner:]
    for part in range(norm.shape[1] // lanes):
        out[start + 12 + part : start + 13 + part, :] = norm[
            0:1, part * lanes : (part + 1) * lanes
        ]


def block_out_body(scal, *refs):
    total = refs[0][...].astype(F32)
    for ref in refs[1:-1]:
        total = total + ref[...].astype(F32)
    refs[-1][...] = total.astype(BF)


def per_device(
    hidden_in,
    out_grad,
    norm_gain,
    gate_weight,
    value_weight,
    step_weight,
    state_weight,
    value_taps,
    value_bias,
    state_taps,
    state_bias,
    step_bias,
    decay_log,
    skip_gain,
    gate_gain,
    out_weight,
):
    heads = lax.axis_size("head")
    count = lax.axis_size("seq")
    head_id = lax.axis_index("head")
    seq_id = lax.axis_index("seq")
    tokens, width = hidden_in.shape
    features = norm_gain.shape[0]
    inner = gate_weight.shape[1]
    local_heads = step_weight.shape[1]
    mixed = inner + 2 * STATE
    chunks = tokens // SPAN
    around = jnp.arange(heads, dtype=jnp.int32)
    order = seq_id.astype(jnp.int32) ^ jnp.asarray(reversed_bits(count), jnp.int32)
    scal = jnp.concatenate(
        [(head_id + around) % heads, (head_id - around) % heads, order, seq_id.reshape(1)]
    ).astype(jnp.int32)

    weights = jnp.concatenate(
        [
            gate_weight,
            value_weight,
            state_weight,
            jnp.pad(step_weight, ((0, 0), (0, LANES - local_heads))),
        ],
        1,
    )
    taps = jnp.concatenate([value_taps, state_taps], 1)
    bias = jnp.concatenate([value_bias, state_bias])[None, :]
    rows8 = jnp.pad(jnp.stack([step_bias, decay_log]), ((0, 6), (0, LANES - local_heads)))
    skip = jnp.repeat(skip_gain, inner // local_heads)[None, :]
    gain = norm_gain[None, :]
    out_gain = gate_gain[None, :]
    expand = (
        jnp.arange(LANES)[:, None] == (jnp.arange(inner) // (inner // local_heads))[None, :]
    ).astype(BF)
    lower = (jnp.arange(SPAN)[:, None] >= jnp.arange(SPAN)[None, :]).astype(BF)

    pieces = [hidden_in] + [cyclic(hidden_in, "head", k) for k in range(1, heads)]
    edge = hidden_in[tokens - 16 :]
    earlier = []
    for k in range(heads):
        routes = [
            (block * heads + place, (block + 1) * heads + (place + k) % heads)
            for block in range(count - 1)
            for place in range(heads)
        ]
        earlier.append(lax.ppermute(edge, ("seq", "head"), routes))
    held, *_ = lax.optimization_barrier((out_grad, *pieces[1:]))
    (
        scal,
        weights,
        taps,
        bias,
        rows8,
        skip,
        gain,
        out_gain,
        expand,
        lower,
        *pieces,
    ) = lax.optimization_barrier(
        (scal, weights, taps, bias, rows8, skip, gain, out_gain, expand, lower, *pieces)
    )
    grad_pieces = [out_grad] + [cyclic(held, "head", k) for k in range(1, heads)]

    def rows_block(columns, size=SPAN):
        return pl.BlockSpec((size, columns), lambda i, s: (i, 0))

    def rows_back(columns, size=SPAN):
        return pl.BlockSpec((size, columns), lambda i, s: (chunks - 1 - i, 0))

    def kernel(body, grid, in_specs, out_specs, out_shape, **options):
        made = call(body, grid, in_specs, out_specs, out_shape, **options)

        return made

    def wide_block(columns):
        return pl.BlockSpec((256, columns), lambda i, s: (i, 0))

    normed, inv, gate, conv, step_raw, before = kernel(
        functools.partial(project_body, heads),
        (tokens // 256,),
        [wide_block(width)] * heads
        + [whole((16, width))] * heads
        + [whole(gain.shape), whole(weights.shape)],
        [
            wide_block(features),
            wide_block(LANES),
            wide_block(inner),
            wide_block(mixed),
            wide_block(LANES),
            whole((16, mixed)),
        ],
        [
            shape_of((tokens, features), BF),
            shape_of((tokens, LANES), F32),
            shape_of((tokens, inner), BF),
            shape_of((tokens, mixed), BF),
            shape_of((tokens, LANES), BF),
            shape_of((16, mixed), BF),
        ],
        flops=2 * tokens * features * weights.shape[1],
        moved=8 * 2**20,
    )(scal, *pieces, *earlier, gain, weights)

    act, slope, step, cum, rows, adds, payload = kernel(
        recur_body,
        (chunks,),
        [
            rows_block(mixed),
            whole((16, mixed)),
            rows_block(LANES),
            whole(taps.shape),
            whole(bias.shape),
            whole(rows8.shape),
            whole(expand.shape),
            whole(lower.shape),
        ],
        [
            rows_block(mixed),
            rows_block(mixed),
            rows_block(LANES),
            rows_block(LANES),
            pl.BlockSpec((16, SPAN), lambda i, s: (i, 0)),
            pl.BlockSpec((1, STATE, inner), lambda i, s: (i, 0, 0)),
            whole((STATE + 16, inner)),
        ],
        [
            shape_of((tokens, mixed), F32),
            shape_of((tokens, mixed), F32),
            shape_of((tokens, LANES), F32),
            shape_of((tokens, LANES), F32),
            shape_of((16 * chunks, SPAN), F32),
            shape_of((chunks, STATE, inner), F32),
            shape_of((STATE + 16, inner), BF),
        ],
        scratch=[
            pltpu.VMEM((SPAN + 8, mixed), F32),
            pltpu.VMEM((STATE, inner), F32),
            pltpu.VMEM((8, LANES), F32),
        ],
        flops=2 * tokens * STATE * inner,
        moved=8 * 2**20,
    )(scal, conv, before, step_raw, taps, bias, rows8, expand, lower)

    incoming = chain(payload, scal, False)

    small_rows = pl.BlockSpec((16, SPAN), lambda i, s: (i, 0))
    (local,) = kernel(
        inside_body,
        (chunks,),
        [rows_block(mixed), rows_block(LANES), small_rows, whole(skip.shape)],
        [rows_block(inner)],
        [shape_of((tokens, inner), F32)],
        flops=2 * tokens * SPAN * inner,
        moved=8 * 2**20,
    )(scal, act, cum, rows, skip)

    grads, back = kernel(
        functools.partial(back_gate_body, heads),
        (chunks,),
        [rows_block(width)] * heads + [whole(out_weight.shape)],
        [rows_block(features), rows_block(inner)],
        [shape_of((tokens, features), BF), shape_of((tokens, inner), F32)],
        flops=2 * tokens * inner * features,
        moved=4 * 2**20,
    )(scal, *grad_pieces, out_weight)

    chunk_state = pl.BlockSpec((1, STATE, inner), lambda i, s: (i, 0, 0))
    mixed_rows, states, sums = kernel(
        mix_body,
        (chunks,),
        [
            rows_block(mixed),
            rows_block(LANES),
            rows_block(inner),
            chunk_state,
            whole((STATE, inner)),
            rows_block(inner),
            rows_block(inner),
            whole(out_gain.shape),
            whole(expand.shape),
        ],
        [rows_block(inner), chunk_state, pl.BlockSpec((8, SPAN), lambda i, s: (0, i))],
        [
            shape_of((tokens, inner), F32),
            shape_of((chunks, STATE, inner), F32),
            shape_of((8, tokens), F32),
        ],
        scratch=[pltpu.VMEM((STATE, inner), F32)],
        flops=2 * tokens * STATE * inner,
        moved=8 * 2**20,
    )(scal, act, cum, local, adds, incoming, gate, back, out_gain, expand)

    totals = [sums] + [cyclic(sums, "head", k) for k in range(1, heads)]

    sums_back = pl.BlockSpec((8, SPAN), lambda i, s: (0, chunks - 1 - i))
    made = kernel(
        functools.partial(gated_back_body, heads),
        (chunks,),
        [sums_back] * heads
        + [
            rows_back(mixed),
            rows_back(LANES),
            rows_back(inner),
            rows_back(inner),
            rows_back(inner),
            whole(out_gain.shape),
            whole(expand.shape),
            whole(out_weight.shape),
        ],
        [rows_back(width)] * heads
        + [
            rows_back(inner),
            rows_back(inner),
            rows_back(inner),
            whole((8, inner)),
            whole((STATE + 16, inner)),
        ],
        [shape_of((tokens, width), F32)]
        + [shape_of((tokens, width), BF)] * (heads - 1)
        + [
            shape_of((tokens, inner), BF),
            shape_of((tokens, inner), BF),
            shape_of((tokens, inner), F32),
            shape_of((8, inner), F32),
            shape_of((STATE + 16, inner), BF),
        ],
        scratch=[pltpu.VMEM((STATE, inner), F32), pltpu.VMEM((8, LANES), F32)],
        flops=2 * tokens * inner * features,
        moved=8 * 2**20,
    )(scal, *totals, act, cum, mixed_rows, gate, back, out_gain, expand, out_weight)
    own_out, sent_out = made[0], made[1:heads]
    normed_gate, gate_part, grad_mixed, gain_grad, back_payload = made[heads:]

    outgoing = chain(back_payload, scal, True)

    out_terms = [cyclic(sent_out[k - 1], "head", k) for k in range(1, heads)]
    (block_out,) = single(
        block_out_body,
        scal,
        [hidden_in, own_out, *out_terms],
        [shape_of((tokens, width), BF)],
        far=(0,),
    )

    values1, maps1, small1 = kernel(
        inside_back_body,
        (chunks,),
        [rows_block(mixed), rows_block(LANES), small_rows, rows_block(inner)],
        [rows_block(inner), rows_block(2 * STATE), rows_block(2 * LANES)],
        [
            shape_of((tokens, inner), F32),
            shape_of((tokens, 2 * STATE), F32),
            shape_of((tokens, 2 * LANES), F32),
        ],
        flops=4 * tokens * SPAN * inner,
        moved=8 * 2**20,
    )(scal, act, cum, rows, grad_mixed)

    groups = features // LANES
    paired = groups == count
    blocked = paired and (LANES // heads) % 16 == 0
    if paired:
        column_scal = scal
    else:
        column_scal = jnp.concatenate([scal[: 2 * heads], jnp.arange(groups, dtype=jnp.int32)])

    def stack_of(size):
        return (groups // 2, size, LANES)

    early_stack = stack_of(2 * inner)
    early_keep, early_send = kernel(
        functools.partial(early_body, heads, groups),
        (1,),
        [whole((tokens, inner)), whole((tokens, features))] * 2,
        [whole(early_stack)] * 2,
        [shape_of(early_stack, BF)] * 2,
        scratch=[pltpu.VMEM((2 * inner, features), F32)],
        flops=4 * tokens * inner * features,
        moved=6 * 2**20,
    )(column_scal, gate_part, normed, normed_gate, grads)

    per_span = SPAN // 16
    back_state = pl.BlockSpec((1, STATE, inner), lambda i, s: (chunks - 1 - i, 0, 0))
    value_part, maps_part, step_part, last_rows, first_rows, tap_grads, small_grads = kernel(
        recur_back_body,
        (chunks,),
        [
            rows_back(mixed),
            rows_back(mixed),
            rows_back(mixed),
            pl.BlockSpec(
                (16, mixed), lambda i, s: (jnp.maximum((chunks - 1 - i) * per_span - 1, 0), 0)
            ),
            whole((16, mixed)),
            rows_back(LANES),
            rows_back(LANES),
            rows_back(LANES),
            rows_back(inner),
            rows_back(inner),
            rows_back(2 * STATE),
            rows_back(2 * LANES),
            back_state,
            whole((STATE, inner)),
            whole(taps.shape),
            whole(rows8.shape),
            whole(skip.shape),
            whole(expand.shape),
            whole(lower.shape),
        ],
        [
            rows_back(inner),
            rows_back(2 * STATE),
            rows_back(LANES),
            whole((16, mixed)),
            whole((8, mixed)),
            whole((8, mixed)),
            whole((8, LANES)),
        ],
        [
            shape_of((tokens, inner), BF),
            shape_of((tokens, 2 * STATE), F32),
            shape_of((tokens, LANES), BF),
            shape_of((16, mixed), F32),
            shape_of((8, mixed), F32),
            shape_of((8, mixed), F32),
            shape_of((8, LANES), F32),
        ],
        scratch=[
            pltpu.VMEM((STATE, inner), F32),
            pltpu.VMEM((SPAN + 8, mixed), F32),
            pltpu.VMEM((SPAN + 8, mixed), F32),
        ],
        flops=8 * tokens * STATE * inner,
        moved=16 * 2**20,
    )(
        scal,
        act,
        slope,
        conv,
        conv,
        before,
        step,
        cum,
        step_raw,
        grad_mixed,
        values1,
        maps1,
        small1,
        states,
        outgoing,
        taps,
        rows8,
        skip,
        expand,
        lower,
    )

    ahead = neighbour(first_rows, "seq", -1)
    part_rows = tokens // heads

    packed = features + 2 * STATE
    late_stack = stack_of(inner + 2 * STATE + 16)
    late_keep, late_send, fixed_part, fixed_maps = kernel(
        functools.partial(late_body, heads, groups),
        (1,),
        [
            whole((tokens, inner)),
            whole((tokens, LANES)),
            whole((tokens, 2 * STATE)),
            whole((16, mixed)),
            whole((8, mixed)),
            whole(taps.shape),
            whole((tokens, features)),
        ],
        [whole(late_stack)] * 2 + [whole((tokens, inner)), whole((tokens, 2 * STATE))],
        [shape_of(late_stack, BF)] * 2
        + [shape_of((tokens, inner), BF), shape_of((tokens, 2 * STATE), BF)],
        scratch=[pltpu.VMEM((late_stack[1], features), F32), pltpu.VMEM((24, mixed), F32)],
        flops=2 * tokens * late_stack[1] * features,
        moved=6 * 2**20,
    )(column_scal, value_part, step_part, maps_part, last_rows, ahead, taps, normed)

    made = single(
        functools.partial(rows_back_body, heads),
        scal,
        [gate_part, fixed_part, step_part, fixed_maps, weights, inv, *pieces],
        [shape_of((part_rows, packed), F32)]
        + [shape_of((part_rows, packed), BF)] * (heads - 1)
        + [shape_of((8, features), F32)],
        scratch=[pltpu.VMEM((tokens, features), F32)] * 2,
    )
    norm_grad = made[heads]
    back_parts = [made[0]] + [cyclic(made[k], "head", k) for k in range(1, heads)]

    if paired:
        grad_gate_weight, grad_out_weight = single(
            early_end_body,
            scal,
            scatter_terms(early_keep, early_send, scal),
            [shape_of((LANES, inner), F32), shape_of((inner, LANES), F32)],
            far=(0, 1),
        )
        grad_value_weight, grad_step_weight, late_maps = single(
            late_end_body,
            scal,
            scatter_terms(late_keep, late_send, scal),
            [
                shape_of((LANES, inner), F32),
                shape_of((LANES, LANES), F32),
                shape_of((LANES, 2 * STATE), F32),
            ],
            far=(0, 1),
        )
        grad_step_weight = grad_step_weight[:, :local_heads]
        if not blocked:
            grad_shared = lax.psum(late_maps, "head")
            piece = LANES // heads
            grad_shared = lax.dynamic_slice_in_dim(grad_shared, head_id * piece, piece, 0)
    else:

        def columns(keep, send, first, last):
            stack = jnp.concatenate([keep, send])[:, first:last].astype(F32)
            return jnp.concatenate(list(stack), 1)

        scatter = functools.partial(lax.psum_scatter, axis_name="seq", tiled=True)
        grad_gate_weight = scatter(columns(early_keep, early_send, 0, inner).T, scatter_dimension=0)
        grad_out_weight = scatter(
            columns(early_keep, early_send, inner, 2 * inner), scatter_dimension=1
        )
        grad_value_weight = scatter(columns(late_keep, late_send, 0, inner).T, scatter_dimension=0)
        first = inner + 2 * STATE
        grad_step_weight = scatter(
            columns(late_keep, late_send, first, first + local_heads).T, scatter_dimension=0
        )
        grad_shared = lax.psum_scatter(
            columns(late_keep, late_send, inner, first).T,
            ("seq", "head"),
            scatter_dimension=0,
            tiled=True,
        )

    lanes = 2 * STATE

    pack_rows = (CONV + 2) * (inner // lanes) + 20
    pack_rows = pack_rows + (-pack_rows) % 8
    (pack,) = single(
        pack_body,
        scal,
        [tap_grads, gain_grad, small_grads, norm_grad],
        [shape_of((pack_rows, lanes), F32)],
    )
    summed = total_sum(pack, "seq", scal)

    own_rows = lambda columns: pl.BlockSpec((part_rows, columns), lambda i, s: (s[0], 0))
    piece = LANES // heads
    size = part_rows + 32 + (2 * piece if blocked else 0)
    late_args = [late_maps] if blocked else []
    final_parts = kernel(
        functools.partial(input_back_body, heads, blocked),
        (1,),
        [whole((part_rows, packed))] * heads
        + [own_rows(width)] * heads
        + [
            own_rows(features),
            own_rows(LANES),
            whole(gain.shape),
            whole(state_weight.shape),
            whole(summed.shape),
        ]
        + [whole(arg.shape) for arg in late_args],
        [whole((size, width))] * heads + [whole((CONV, inner)), whole((8, inner))],
        [shape_of((size, width), BF)] * heads
        + [shape_of((CONV, inner), F32), shape_of((8, inner), F32)],
        scratch=[pltpu.VMEM((part_rows, features), F32)],
        flops=2 * tokens * features,
        moved=4 * 2**20,
        far=(heads, heads + 1),
    )(scal, *back_parts, *pieces, grads, inv, gain, state_weight, summed, *late_args)
    grad_value_taps, rest = final_parts[heads:]
    finals = [final_parts[0]] + [cyclic(final_parts[k], "head", k) for k in range(1, heads)]

    made = kernel(
        functools.partial(finish_body, heads),
        (1,),
        [whole((size, width))] * heads,
        [whole((tokens, width)), whole((16, lanes))] + ([whole((piece, lanes))] if blocked else []),
        [shape_of((tokens, width), BF), shape_of((16, lanes), F32)]
        + ([shape_of((piece, lanes), F32)] if blocked else []),
        flops=2 * tokens * features,
        moved=2**20,
        far=(0, 1, 2) if blocked else (0, 1),
    )(scal, *finals)
    grad_in, shared_small = made[:2]
    if blocked:
        grad_shared = made[2]
    return (
        block_out,
        grad_in,
        shared_small[8 : 8 + features // lanes].reshape(-1),
        grad_gate_weight,
        grad_value_weight,
        grad_step_weight,
        grad_shared,
        grad_value_taps,
        rest[0],
        shared_small[:CONV],
        shared_small[CONV],
        rest[2, :local_heads],
        rest[3, :local_heads],
        rest[4, :local_heads],
        rest[1],
        grad_out_weight,
    )


def solution(mesh):
    in_specs = (
        P("seq", "head"),
        P("seq", "head"),
        P(),
        P(None, "head"),
        P(None, "head"),
        P(None, "head"),
        P(),
        P(None, "head"),
        P("head"),
        P(),
        P(),
        P("head"),
        P("head"),
        P("head"),
        P("head"),
        P("head", None),
    )
    out_specs = (
        P("seq", "head"),
        P("seq", "head"),
        P(),
        P("seq", "head"),
        P("seq", "head"),
        P("seq", "head"),
        P(("seq", "head"), None),
        P(None, "head"),
        P("head"),
        P(),
        P(),
        P("head"),
        P("head"),
        P("head"),
        P("head"),
        P("head", "seq"),
    )

    return jax.shard_map(
        per_device, mesh=mesh, in_specs=in_specs, out_specs=out_specs, check_vma=False
    )
```
